512 devices in a mesh: row: 16 (over x, z_hi, core), col: 32 (over y, z_lo).
Axes of the slice: x: 4, y: 4, z: 16 (z_hi: 2, z_lo: 8; z = z_hi * 8 + z_lo), core: 2. Of those that a mesh axis runs over, the one named last changes fastest.
Arguments:
- a_blocks: float32 [384, 16, 128, 128], P('col', 'row'), may hold values from -0.25 to 0.25
- a_cols: int32 [384, 16], P('col'), may hold values from 0 to 63, as said below
- a_lengths: int32 [384], P('col'), may hold values from 1 to 16, as said below
- b_blocks: float32 [64, 16, 128, 128], P('col', 'row'), may hold values from -6 to 6
- b_cols: int32 [64, 16], P(None, 'row'), may hold values from 0 to 7
- c_cols: int32 [384, 64], P('col', 'row'), may hold values from 0 to 7, as said below
- order: int32 [64], replicated, may hold values from 0 to 63, each once
Outputs:
- c_blocks: float32 [384, 64, 128, 128], P('col', 'row')
The draws below stay inside these ranges and needn't reach their ends.
Inputs may be any that keep to these rules, and one draw needn't show every extreme that they name: `a_cols`: the 16 entries of one row are distinct. `a_lengths`: the first row has 16 live slots; slots at or after a row's length hold blocks that are not used. `c_cols`: the 4 entries of one row in one row group are distinct. `order`: each number once.
All inputs are finite; a program needn't handle non-finite values.
Results may differ from the reference program's by a relative error of at most 0.0003.
Values sent between devices are 32-bit elements; how exact they have to be, the bound alone decides.
No kernel may reach another device: no remote copies, remote signals or barrier semaphores. Data moves between devices by JAX's collectives and lax.ppermute only.
A program may use at most 64 MiB of HBM per device.

```python
import jax
import jax.numpy as jnp
from jax import lax

BLOCK = 128
SLOTS = 16
ROWS_DEV = 12
WIN = 8
CSLOTS = 4
ROWS = 384
NACT = 64
C_ALL = 64
N_ROW = 16


def draw_a_cols(key, part):
    scores = jax.random.randint(key, (ROWS, NACT), 0, 65536) * NACT + jnp.arange(NACT, dtype=jnp.int32)[None, :]
    ranked = jnp.argsort(scores, axis=-1)
    return ranked[:, :SLOTS].astype(jnp.int32)


def draw_a_lengths(key, part):
    first_key = jax.random.fold_in(key, 11)
    second_key = jax.random.fold_in(key, 23)
    level_code = jax.random.randint(first_key, (ROWS // ROWS_DEV,), 0, 8)
    level = jnp.where(level_code == 7, 4, jnp.where(level_code == 6, 2, 1))
    level_rows = jnp.repeat(level, ROWS_DEV)
    jitter = jax.random.randint(second_key, (ROWS,), 0, SLOTS // 8 + 1)
    lengths = jnp.clip(level_rows * (SLOTS // 4) - jitter, 1, SLOTS)
    lengths = lengths.at[0].set(SLOTS)
    return lengths.astype(jnp.int32)


def draw_c_cols(key, part):
    group_count = C_ALL // CSLOTS
    scores = jax.random.randint(key, (ROWS, group_count, WIN), 0, 65536) * WIN + jnp.arange(WIN, dtype=jnp.int32)
    ranked = jnp.argsort(scores, axis=-1)
    return ranked[:, :, :CSLOTS].reshape(ROWS, C_ALL).astype(jnp.int32)


def touch_ends(values, key, low, largest):
    longest = values.shape.index(max(values.shape))
    spots = []
    for shift in (0, 1):
        where = [jax.random.randint(jax.random.fold_in(key, axis), (), 0, length) for axis, length in enumerate(values.shape)]
        where[longest] = (where[longest] + shift) % values.shape[longest]
        spots.append(tuple(where))
    return values.at[spots[0]].set(low).at[spots[1]].set(largest)


def block_scale(own_key, shape, shards, smallest, high):
    gain, own = 1.0, jax.random.fold_in(own_key, 6)
    for dim, blocks in shards:
        draws = jnp.exp(jax.random.uniform(jax.random.fold_in(own, dim), (blocks,), jnp.float32, smallest / len(shards), high / len(shards)))
        gain = gain * jnp.repeat(draws, shape[dim] // blocks).reshape([-1 if axis == dim else 1 for axis in range(len(shape))])
    return gain


def bell_draw(rng, dims, deviation, bound, cuts=(), kind=jnp.bfloat16):
    level = block_scale(rng, dims, cuts, -0.22, 0.18) if cuts else 1.0
    array = jax.random.normal(rng, dims, jnp.float32) * deviation * level
    return jnp.minimum(jnp.maximum(array, -bound), bound).astype(kind)


def setup_inputs(seed: int = 0) -> dict:
    arg_keys = jax.random.split(jax.random.key(seed), 8)
    a_blocks = bell_draw(arg_keys[0], (ROWS, SLOTS, BLOCK, BLOCK), (BLOCK * 4) ** -0.5, 0.25, ((0, 32), (1, 16)), jnp.float32)
    a_cols = draw_a_cols(jax.random.fold_in(arg_keys[7], 71), 0)
    a_lengths = draw_a_lengths(jax.random.fold_in(arg_keys[7], 71), 0)
    b_blocks = bell_draw(arg_keys[3], (NACT, N_ROW, BLOCK, BLOCK), 1.0, 6.0, ((0, 32), (1, 16)), jnp.float32)
    b_cols = touch_ends(jax.random.randint(arg_keys[4], (NACT, N_ROW), 0, WIN), jax.random.fold_in(arg_keys[4], 1), 0, WIN - 1).astype(jnp.int32)
    c_cols = draw_c_cols(jax.random.fold_in(arg_keys[7], 71), 0)
    order = jax.random.permutation(arg_keys[6], NACT).astype(jnp.int32)
    return {"a_blocks": a_blocks, "a_cols": a_cols, "a_lengths": a_lengths, "b_blocks": b_blocks, "b_cols": b_cols, "c_cols": c_cols, "order": order}


def reference(a_blocks, a_cols, a_lengths, b_blocks, b_cols, c_cols, order):
    position = order[a_cols]
    live_slots = jnp.arange(SLOTS, dtype=jnp.int32)[None, :] < a_lengths[:, None]
    group_count = c_cols.shape[1] // CSLOTS

    def one_row(packed):
        a_row, pos_row, live_row, pattern = packed
        chosen = b_blocks[pos_row].astype(jnp.float32)
        chosen_cols = b_cols[pos_row]
        pattern_two = pattern.reshape(group_count, CSLOTS)
        matches = (chosen_cols[:, :, None] == pattern_two[None, :, :]) & live_row[:, None, None]
        matches = matches.astype(jnp.float32)
        products = jnp.einsum("jab,jgbc->jgac", a_row.astype(jnp.float32), chosen,
                              precision=lax.Precision.HIGHEST)
        summed = jnp.einsum("jgs,jgac->gsac", matches, products, precision=lax.Precision.HIGHEST)
        return summed.reshape(group_count * CSLOTS, BLOCK, BLOCK)

    return lax.map(one_row, (a_blocks, position, live_slots, c_cols))
```

```python
import functools

import jax
import jax.numpy as jnp
from jax import lax
from jax.sharding import PartitionSpec as P


def lookup(values_table, indices):
    matched = indices[..., None] == jnp.arange(values_table.shape[0], dtype=jnp.int32)
    return jnp.sum(jnp.where(matched, values_table, 0), axis=-1)


def row_gather(chunk, n_row):
    n_x = n_row // 4
    swap_z = [(r, r ^ 2) for r in range(n_row)]
    held = jnp.concatenate([chunk, lax.ppermute(chunk, "row", swap_z)], axis=1)
    parts = [held]
    for k in range(1, n_x):
        shift = [(r, ((r // 4 + k) % n_x) * 4 + r % 4) for r in range(n_row)]
        parts.append(lax.ppermute(held, "row", shift))
    held = jnp.concatenate(parts, axis=1)
    swap_core = [(r, r ^ 1) for r in range(n_row)]
    return jnp.concatenate([held, lax.ppermute(held, "row", swap_core)], axis=1)


def row_slot_of_held(n_row):
    n_x = n_row // 4
    r = lax.axis_index("row")
    x, zh, core = r // 4, (r // 2) % 2, r % 2
    h = jnp.arange(n_row, dtype=jnp.int32)
    cb, k, zb = h // (2 * n_x), (h // 2) % n_x, h % 2
    return ((x - k) % n_x) * 4 + (zh ^ zb) * 2 + (core ^ cb)


def col_gather(chunk, n_col):
    n_y = n_col // 8
    parts = [chunk]
    for k in range(1, 8):
        shift = [(c, (c // 8) * 8 + (c % 8 + k) % 8) for c in range(n_col)]
        parts.append(lax.ppermute(chunk, "col", shift))
    held = jnp.concatenate(parts, axis=0)
    parts = [held]
    for k in range(1, n_y):
        shift = [(c, ((c // 8 + k) % n_y) * 8 + c % 8) for c in range(n_col)]
        parts.append(lax.ppermute(held, "col", shift))
    return jnp.concatenate(parts, axis=0)


def col_held_index(grid_pos, per_dev, n_col):
    n_y = n_col // 8
    c = lax.axis_index("col")
    y, zl = c // 8, c % 8
    src = grid_pos // per_dev
    return ((y - src // 8) % n_y) * (8 * per_dev) + ((zl - src % 8) % 8) * per_dev + grid_pos % per_dev


def local(a_blocks, a_cols, a_lengths, b_blocks, b_cols, c_cols, order, n_row, n_col):
    per_dev = b_blocks.shape[0]
    panels = col_gather(b_blocks[:, 0], n_col)
    rows_here, slot_all = a_cols.shape
    pattern_slots = c_cols.shape[1]
    block_size = panels.shape[-1]
    slot_of_held = row_slot_of_held(n_row)
    position = jnp.take(lookup(order, a_cols), slot_of_held, axis=1)
    window_col = lookup(b_cols[:, 0], position)
    panel_index = col_held_index(position, per_dev, n_col)
    live_slots = slot_of_held[None, :] < a_lengths[:, None]
    weights = ((window_col[:, :, None] == c_cols[:, None, :]) & live_slots[:, :, None]).astype(
        jnp.float32
    )
    zero_sums = jnp.zeros((rows_here, pattern_slots, block_size, block_size), jnp.float32)
    whole_slots = row_gather(a_blocks, n_row)

    def per_row(row_index, running):
        chosen = jnp.take(panels, panel_index[row_index], axis=0)
        products = jnp.einsum(
            "jab,jbc->jac", whole_slots[row_index], chosen, precision=lax.Precision.HIGHEST
        )
        landed = jnp.einsum(
            "js,jac->sac", weights[row_index], products, precision=lax.Precision.HIGHEST
        )
        return running.at[row_index].add(landed)

    return lax.fori_loop(0, rows_here, per_row, zero_sums)


def solution(mesh):
    sizes = dict(n_row=mesh.shape["row"], n_col=mesh.shape["col"])
    return jax.shard_map(
        functools.partial(local, **sizes),
        mesh=mesh,
        in_specs=(
            P("col", "row", None, None),
            P("col", None),
            P("col"),
            P("col", "row", None, None),
            P(None, "row"),
            P("col", "row"),
            P(),
        ),
        out_specs=P("col", "row", None, None),
        check_vma=False,
    )
```

```python
import functools

import jax
import jax.numpy as jnp
from jax import lax
from jax.experimental import pallas as pl
from jax.experimental.pallas import tpu as pltpu
from jax.sharding import PartitionSpec as P


def lookup(values_table, indices):
    matched = indices[..., None] == jnp.arange(values_table.shape[0], dtype=jnp.int32)
    return jnp.sum(jnp.where(matched, values_table, 0), axis=-1)


def row_stages(n_row):
    n_x = n_row // 4

    def swap_z(chunk):
        pairs = [(r, r ^ 2) for r in range(n_row)]
        return jnp.concatenate([chunk, lax.ppermute(chunk, "row", pairs)], axis=1)

    def ring_x(held):
        parts = [held]
        for k in range(1, n_x):
            shift = [(r, ((r // 4 + k) % n_x) * 4 + r % 4) for r in range(n_row)]
            parts.append(lax.ppermute(held, "row", shift))
        return jnp.concatenate(parts, axis=1)

    def swap_core(held):
        pairs = [(r, r ^ 1) for r in range(n_row)]
        return jnp.concatenate([held, lax.ppermute(held, "row", pairs)], axis=1)

    return swap_z, ring_x, swap_core


def row_slot_of_held(n_row):
    n_x = n_row // 4
    r = lax.axis_index("row")
    x, zh, core = r // 4, (r // 2) % 2, r % 2
    h = jnp.arange(n_row, dtype=jnp.int32)
    cb, k, zb = h // (2 * n_x), (h // 2) % n_x, h % 2
    return ((x - k) % n_x) * 4 + (zh ^ zb) * 2 + (core ^ cb)


def col_stages(n_col):
    n_y = n_col // 8

    def line_z(chunk):
        parts = [chunk]
        for k in range(1, 8):
            shift = [(c, (c // 8) * 8 + (c % 8 + k) % 8) for c in range(n_col)]
            parts.append(lax.ppermute(chunk, "col", shift))
        return jnp.concatenate(parts, axis=0)

    def ring_y(held):
        parts = [held]
        for k in range(1, n_y):
            shift = [(c, ((c // 8 + k) % n_y) * 8 + c % 8) for c in range(n_col)]
            parts.append(lax.ppermute(held, "col", shift))
        return jnp.concatenate(parts, axis=0)

    return line_z, ring_y


def col_held_index(grid_pos, per_dev, n_col):
    n_y = n_col // 8
    c = lax.axis_index("col")
    y, zl = c // 8, c % 8
    src = grid_pos // per_dev
    return ((y - src // 8) % n_y) * (8 * per_dev) + ((zl - src % 8) % 8) * per_dev + grid_pos % per_dev


def local(a_blocks, a_cols, a_lengths, b_blocks, b_cols, c_cols, order, n_row, n_col):
    per_dev = b_blocks.shape[0]
    swap_z, ring_x, swap_core = row_stages(n_row)
    line_z, ring_y = col_stages(n_col)
    a_held, b_held = lax.optimization_barrier((swap_z(a_blocks), line_z(b_blocks[:, 0])))
    a_held, panels = lax.optimization_barrier((ring_x(a_held), ring_y(b_held)))
    whole_slots = swap_core(a_held)
    rows_here, slot_all = a_cols.shape
    pattern_slots = c_cols.shape[1]
    block_size = panels.shape[-1]
    slot_of_held = row_slot_of_held(n_row)
    position = jnp.take(lookup(order, a_cols), slot_of_held, axis=1)
    window_col = lookup(b_cols[:, 0], position)
    panel_index = col_held_index(position, per_dev, n_col)
    live_slots = slot_of_held[None, :] < a_lengths[:, None]
    weights = ((window_col[:, :, None] == c_cols[:, None, :]) & live_slots[:, :, None]).astype(
        jnp.float32
    )
    target = jnp.where(jnp.any(weights > 0, axis=-1), jnp.argmax(weights, axis=-1), -1)
    return row_products(whole_slots, panels, panel_index.reshape(-1), target.astype(jnp.int32).reshape(-1), pattern_slots)


def product_kernel(pidx_ref, sidx_ref, a_ref, b_ref, o_ref):
    i = pl.program_id(0)
    n_slots = a_ref.shape[1]
    o_ref[...] = jnp.zeros_like(o_ref)

    def body(j, carry):
        s = sidx_ref[i * n_slots + j]

        @pl.when(s >= 0)
        def _():
            p = pidx_ref[i * n_slots + j]
            prod = jnp.dot(a_ref[0, j], b_ref[p], precision=lax.Precision.HIGHEST,
                           preferred_element_type=jnp.float32)
            o_ref[0, s] += prod

        return carry

    lax.fori_loop(0, n_slots, body, 0)


def row_products(whole_slots, panels, panel_index, target, pattern_slots, interpret=False):
    rows, slots, bs, _ = whole_slots.shape
    grid_spec = pltpu.PrefetchScalarGridSpec(
        num_scalar_prefetch=2,
        grid=(rows,),
        in_specs=[
            pl.BlockSpec((1, slots, bs, bs), lambda i, pidx, sidx: (i, 0, 0, 0)),
            pl.BlockSpec(panels.shape, lambda i, pidx, sidx: (0, 0, 0)),
        ],
        out_specs=pl.BlockSpec((1, pattern_slots, bs, bs), lambda i, pidx, sidx: (i, 0, 0, 0)),
    )
    return pl.pallas_call(
        product_kernel,
        grid_spec=grid_spec,
        out_shape=jax.ShapeDtypeStruct((rows, pattern_slots, bs, bs), jnp.float32),
        interpret=interpret,
    )(panel_index, target, whole_slots, panels)


def solution(mesh):
    sizes = dict(n_row=mesh.shape["row"], n_col=mesh.shape["col"])
    return jax.shard_map(
        functools.partial(local, **sizes),
        mesh=mesh,
        in_specs=(
            P("col", "row", None, None),
            P("col", None),
            P("col"),
            P("col", "row", None, None),
            P(None, "row"),
            P("col", "row"),
            P(),
        ),
        out_specs=P("col", "row", None, None),
        check_vma=False,
    )
```

```python
import functools

import jax
import jax.numpy as jnp
from jax import lax
from jax.experimental import pallas as pl
from jax.experimental.pallas import tpu as pltpu
from jax.sharding import PartitionSpec as P


def lookup(values_table, indices):
    matched = indices[..., None] == jnp.arange(values_table.shape[0], dtype=jnp.int32)
    return jnp.sum(jnp.where(matched, values_table, 0), axis=-1)


def row_stages(n_row):
    n_x = n_row // 4

    def swap_z(chunk):
        pairs = [(r, r ^ 2) for r in range(n_row)]
        return jnp.concatenate([chunk, lax.ppermute(chunk, "row", pairs)], axis=1)

    def ring_x(held):
        parts = [held]
        for k in range(1, n_x):
            shift = [(r, ((r // 4 + k) % n_x) * 4 + r % 4) for r in range(n_row)]
            parts.append(lax.ppermute(held, "row", shift))
        return jnp.concatenate(parts, axis=1)

    def swap_core(held):
        pairs = [(r, r ^ 1) for r in range(n_row)]
        return lax.ppermute(held, "row", pairs)

    return swap_z, ring_x, swap_core


def row_slot_of_held(n_row):
    n_x = n_row // 4
    r = lax.axis_index("row")
    x, zh, core = r // 4, (r // 2) % 2, r % 2
    h = jnp.arange(n_row, dtype=jnp.int32)
    cb, k, zb = h // (2 * n_x), (h // 2) % n_x, h % 2
    return ((x - k) % n_x) * 4 + (zh ^ zb) * 2 + (core ^ cb)


def col_stages(n_col):
    n_y = n_col // 8

    def line_z(chunk):
        c = lax.axis_index("col")
        zl = c % 8
        right = [(c, c + 1) for c in range(n_col) if c % 8 < 7]
        left = [(c, c - 1) for c in range(n_col) if c % 8 > 0]
        from_left, from_right = [chunk], []
        going_right, going_left = chunk, chunk
        for _ in range(7):
            going_right = lax.ppermute(going_right, "col", right)
            going_left = lax.ppermute(going_left, "col", left)
            from_left.append(going_right)
            from_right.append(going_left)
        pieces = jnp.stack(from_left + from_right, axis=0)
        src = jnp.arange(8, dtype=jnp.int32)
        pick = jnp.where(src <= zl, zl - src, 7 + src - zl)
        return jnp.take(pieces, pick, axis=0).reshape((-1,) + chunk.shape[1:])

    def ring_y(held):
        parts = [held]
        for k in range(1, n_y):
            shift = [(c, ((c // 8 + k) % n_y) * 8 + c % 8) for c in range(n_col)]
            parts.append(lax.ppermute(held, "col", shift))
        return jnp.concatenate(parts, axis=0)

    return line_z, ring_y


def col_held_index(grid_pos, per_dev, n_col):
    n_y = n_col // 8
    c = lax.axis_index("col")
    y = c // 8
    src = grid_pos // per_dev
    return ((y - src // 8) % n_y) * (8 * per_dev) + (src % 8) * per_dev + grid_pos % per_dev


def local(a_blocks, a_cols, a_lengths, b_blocks, b_cols, c_cols, order, n_row, n_col):
    per_dev = b_blocks.shape[0]
    swap_z, ring_x, swap_core = row_stages(n_row)
    line_z, ring_y = col_stages(n_col)
    a_held, b_held = lax.optimization_barrier((swap_z(a_blocks), line_z(b_blocks[:, 0])))
    a_held, panels = lax.optimization_barrier((ring_x(a_held), ring_y(b_held)))
    rows_here, slot_all = a_cols.shape
    pattern_slots = c_cols.shape[1]
    block_size = panels.shape[-1]
    slot_of_held = row_slot_of_held(n_row)
    position = jnp.take(lookup(order, a_cols), slot_of_held, axis=1)
    window_col = lookup(b_cols[:, 0], position)
    panel_index = col_held_index(position, per_dev, n_col)
    live_slots = slot_of_held[None, :] < a_lengths[:, None]
    weights = ((window_col[:, :, None] == c_cols[:, None, :]) & live_slots[:, :, None]).astype(
        jnp.float32
    )
    target = jnp.where(jnp.any(weights > 0, axis=-1), jnp.argmax(weights, axis=-1), -1)
    target = target.astype(jnp.int32)
    half = a_held.shape[1]
    mine = row_products(a_held, panels, panel_index[:, :half].reshape(-1),
                        target[:, :half].reshape(-1), pattern_slots)
    return row_products(swap_core(a_held), panels, panel_index[:, half:].reshape(-1),
                        target[:, half:].reshape(-1), pattern_slots, mine)


def product_kernel(pidx_ref, sidx_ref, a_ref, b_ref, *rest):
    i = pl.program_id(0)
    n_slots = a_ref.shape[1]
    o_ref = rest[-1]
    if len(rest) == 2:
        o_ref[...] = rest[0][...]
    else:
        o_ref[...] = jnp.zeros_like(o_ref)

    def body(j, carry):
        s = sidx_ref[i * n_slots + j]

        @pl.when(s >= 0)
        def _():
            p = pidx_ref[i * n_slots + j]
            prod = jnp.dot(a_ref[0, j], b_ref[p], precision=lax.Precision.HIGHEST,
                           preferred_element_type=jnp.float32)
            o_ref[0, s] += prod

        return carry

    lax.fori_loop(0, n_slots, body, 0)


def row_products(whole_slots, panels, panel_index, target, pattern_slots, acc=None, interpret=False):
    rows, slots, bs, _ = whole_slots.shape
    out_spec = pl.BlockSpec((1, pattern_slots, bs, bs), lambda i, pidx, sidx: (i, 0, 0, 0))
    extra = [] if acc is None else [acc]
    grid_spec = pltpu.PrefetchScalarGridSpec(
        num_scalar_prefetch=2,
        grid=(rows,),
        in_specs=[
            pl.BlockSpec((1, slots, bs, bs), lambda i, pidx, sidx: (i, 0, 0, 0)),
            pl.BlockSpec(panels.shape, lambda i, pidx, sidx: (0, 0, 0)),
        ] + [out_spec] * len(extra),
        out_specs=out_spec,
    )
    return pl.pallas_call(
        product_kernel,
        grid_spec=grid_spec,
        out_shape=jax.ShapeDtypeStruct((rows, pattern_slots, bs, bs), jnp.float32),
        input_output_aliases={} if acc is None else {4: 0},
        interpret=interpret,
    )(panel_index, target, whole_slots, panels, *extra)


def solution(mesh):
    sizes = dict(n_row=mesh.shape["row"], n_col=mesh.shape["col"])
    return jax.shard_map(
        functools.partial(local, **sizes),
        mesh=mesh,
        in_specs=(
            P("col", "row", None, None),
            P("col", None),
            P("col"),
            P("col", "row", None, None),
            P(None, "row"),
            P("col", "row"),
            P(),
        ),
        out_specs=P("col", "row", None, None),
        check_vma=False,
    )
```

```python
import functools

import jax
import jax.numpy as jnp
from jax import lax
from jax.experimental import pallas as pl
from jax.experimental.pallas import tpu as pltpu
from jax.sharding import PartitionSpec as P


def lookup(values_table, indices):
    matched = indices[..., None] == jnp.arange(values_table.shape[0], dtype=jnp.int32)
    return jnp.sum(jnp.where(matched, values_table, 0), axis=-1)


def row_stages(n_row):
    n_x = n_row // 4

    def swap_z(chunk):
        pairs = [(r, r ^ 2) for r in range(n_row)]
        return jnp.concatenate([chunk, lax.ppermute(chunk, "row", pairs)], axis=1)

    def ring_x(held):
        parts = [held]
        for k in range(1, n_x):
            shift = [(r, ((r // 4 + k) % n_x) * 4 + r % 4) for r in range(n_row)]
            parts.append(lax.ppermute(held, "row", shift))
        return jnp.concatenate(parts, axis=1)

    def swap_core(held):
        pairs = [(r, r ^ 1) for r in range(n_row)]
        return lax.ppermute(held, "row", pairs)

    return swap_z, ring_x, swap_core


def row_slot_of_held(n_row):
    n_x = n_row // 4
    r = lax.axis_index("row")
    x, zh, core = r // 4, (r // 2) % 2, r % 2
    h = jnp.arange(n_row, dtype=jnp.int32)
    cb, k, zb = h // (2 * n_x), (h // 2) % n_x, h % 2
    return ((x - k) % n_x) * 4 + (zh ^ zb) * 2 + (core ^ cb)


def col_stages(n_col):
    n_y = n_col // 8

    def line_z(chunk):
        c = lax.axis_index("col")
        zl = c % 8
        right = [(c, c + 1) for c in range(n_col) if c % 8 < 7]
        left = [(c, c - 1) for c in range(n_col) if c % 8 > 0]
        from_left, from_right = [chunk], []
        going_right, going_left = chunk, chunk
        for _ in range(7):
            going_right = lax.ppermute(going_right, "col", right)
            going_left = lax.ppermute(going_left, "col", left)
            from_left.append(going_right)
            from_right.append(going_left)
        pieces = jnp.stack(from_left + from_right, axis=0)
        src = jnp.arange(8, dtype=jnp.int32)
        pick = jnp.where(src <= zl, zl - src, 7 + src - zl)
        return jnp.take(pieces, pick, axis=0).reshape((-1,) + chunk.shape[1:])

    def ring_y(held):
        parts = [held]
        for k in range(1, n_y):
            shift = [(c, ((c // 8 + k) % n_y) * 8 + c % 8) for c in range(n_col)]
            parts.append(lax.ppermute(held, "col", shift))
        return jnp.concatenate(parts, axis=0)

    return line_z, ring_y


def col_held_index(grid_pos, per_dev, n_col):
    n_y = n_col // 8
    c = lax.axis_index("col")
    y = c // 8
    src = grid_pos // per_dev
    return (src % 8) * (n_y * per_dev) + ((y - src // 8) % n_y) * per_dev + grid_pos % per_dev


def local(a_blocks, a_cols, a_lengths, b_blocks, b_cols, c_cols, order, n_row, n_col):
    per_dev = b_blocks.shape[0]
    swap_z, ring_x, swap_core = row_stages(n_row)
    line_z, ring_y = col_stages(n_col)
    a_held, b_held = lax.optimization_barrier((swap_z(a_blocks), ring_y(b_blocks[:, 0])))
    a_held, panels = lax.optimization_barrier((ring_x(a_held), line_z(b_held)))
    rows_here, slot_all = a_cols.shape
    pattern_slots = c_cols.shape[1]
    block_size = panels.shape[-1]
    slot_of_held = row_slot_of_held(n_row)
    position = jnp.take(lookup(order, a_cols), slot_of_held, axis=1)
    window_col = lookup(b_cols[:, 0], position)
    panel_index = col_held_index(position, per_dev, n_col)
    live_slots = slot_of_held[None, :] < a_lengths[:, None]
    weights = ((window_col[:, :, None] == c_cols[:, None, :]) & live_slots[:, :, None]).astype(
        jnp.float32
    )
    target = jnp.where(jnp.any(weights > 0, axis=-1), jnp.argmax(weights, axis=-1), -1)
    target = target.astype(jnp.int32)
    half = a_held.shape[1]
    mine = row_products(a_held, panels, panel_index[:, :half].reshape(-1),
                        target[:, :half].reshape(-1), pattern_slots)
    return row_products(swap_core(a_held), panels, panel_index[:, half:].reshape(-1),
                        target[:, half:].reshape(-1), pattern_slots, mine)


def product_kernel(pidx_ref, sidx_ref, a_ref, b_ref, *rest):
    i = pl.program_id(0)
    n_slots = a_ref.shape[1]
    o_ref = rest[-1]
    if len(rest) == 2:
        o_ref[...] = rest[0][...]
    else:
        o_ref[...] = jnp.zeros_like(o_ref)

    def body(j, carry):
        s = sidx_ref[i * n_slots + j]

        @pl.when(s >= 0)
        def _():
            p = pidx_ref[i * n_slots + j]
            prod = jnp.dot(a_ref[0, j], b_ref[p], precision=lax.Precision.HIGHEST,
                           preferred_element_type=jnp.float32)
            o_ref[0, s] += prod

        return carry

    lax.fori_loop(0, n_slots, body, 0)


def row_products(whole_slots, panels, panel_index, target, pattern_slots, acc=None, interpret=False):
    rows, slots, bs, _ = whole_slots.shape
    out_spec = pl.BlockSpec((1, pattern_slots, bs, bs), lambda i, pidx, sidx: (i, 0, 0, 0))
    extra = [] if acc is None else [acc]
    grid_spec = pltpu.PrefetchScalarGridSpec(
        num_scalar_prefetch=2,
        grid=(rows,),
        in_specs=[
            pl.BlockSpec((1, slots, bs, bs), lambda i, pidx, sidx: (i, 0, 0, 0)),
            pl.BlockSpec(panels.shape, lambda i, pidx, sidx: (0, 0, 0)),
        ] + [out_spec] * len(extra),
        out_specs=out_spec,
    )
    return pl.pallas_call(
        product_kernel,
        grid_spec=grid_spec,
        out_shape=jax.ShapeDtypeStruct((rows, pattern_slots, bs, bs), jnp.float32),
        input_output_aliases={} if acc is None else {4: 0},
        interpret=interpret,
    )(panel_index, target, whole_slots, panels, *extra)


def solution(mesh):
    sizes = dict(n_row=mesh.shape["row"], n_col=mesh.shape["col"])
    return jax.shard_map(
        functools.partial(local, **sizes),
        mesh=mesh,
        in_specs=(
            P("col", "row", None, None),
            P("col", None),
            P("col"),
            P("col", "row", None, None),
            P(None, "row"),
            P("col", "row"),
            P(),
        ),
        out_specs=P("col", "row", None, None),
        check_vma=False,
    )
```

```python
import functools

import jax
import jax.numpy as jnp
from jax import lax
from jax.experimental import pallas as pl
from jax.experimental.pallas import tpu as pltpu
from jax.sharding import PartitionSpec as P


def lookup(values_table, indices):
    matched = indices[..., None] == jnp.arange(values_table.shape[0], dtype=jnp.int32)
    return jnp.sum(jnp.where(matched, values_table, 0), axis=-1)


def row_stages(n_row):
    n_x = n_row // 4

    def swap_z(chunk):
        pairs = [(r, r ^ 2) for r in range(n_row)]
        return jnp.concatenate([chunk, lax.ppermute(chunk, "row", pairs)], axis=1)

    def ring_x(held):
        parts = [held]
        for k in range(1, n_x):
            shift = [(r, ((r // 4 + k) % n_x) * 4 + r % 4) for r in range(n_row)]
            parts.append(lax.ppermute(held, "row", shift))
        return jnp.concatenate(parts, axis=1)

    def swap_core(held):
        pairs = [(r, r ^ 1) for r in range(n_row)]
        return lax.ppermute(held, "row", pairs)

    return swap_z, ring_x, swap_core


def row_slot_of_held(n_row):
    n_x = n_row // 4
    r = lax.axis_index("row")
    x, zh, core = r // 4, (r // 2) % 2, r % 2
    h = jnp.arange(n_row, dtype=jnp.int32)
    cb, k, zb = h // (2 * n_x), (h // 2) % n_x, h % 2
    return ((x - k) % n_x) * 4 + (zh ^ zb) * 2 + (core ^ cb)


def col_stages(n_col):
    n_y = n_col // 8

    def line_z(chunk):
        c = lax.axis_index("col")
        zl = c % 8
        right = [(c, c + 1) for c in range(n_col) if c % 8 < 7]
        left = [(c, c - 1) for c in range(n_col) if c % 8 > 0]
        from_left, from_right = [chunk], []
        going_right, going_left = chunk, chunk
        for _ in range(7):
            going_right = lax.ppermute(going_right, "col", right)
            going_left = lax.ppermute(going_left, "col", left)
            from_left.append(going_right)
            from_right.append(going_left)
        pieces = jnp.stack(from_left + from_right, axis=0)
        src = jnp.arange(8, dtype=jnp.int32)
        pick = jnp.where(src <= zl, zl - src, 7 + src - zl)
        return jnp.take(pieces, pick, axis=0).reshape((-1,) + chunk.shape[1:])

    def ring_y(held):
        parts = [held]
        for k in range(1, n_y):
            shift = [(c, ((c // 8 + k) % n_y) * 8 + c % 8) for c in range(n_col)]
            parts.append(lax.ppermute(held, "col", shift))
        return jnp.concatenate(parts, axis=0)

    return line_z, ring_y


def col_held_index(grid_pos, per_dev, n_col):
    n_y = n_col // 8
    c = lax.axis_index("col")
    y = c // 8
    src = grid_pos // per_dev
    return ((y - src // 8) % n_y) * (8 * per_dev) + (src % 8) * per_dev + grid_pos % per_dev


def local(a_blocks, a_cols, a_lengths, b_blocks, b_cols, c_cols, order, n_row, n_col):
    per_dev = b_blocks.shape[0]
    swap_z, ring_x, swap_core = row_stages(n_row)
    line_z, ring_y = col_stages(n_col)
    a_held, b_held = lax.optimization_barrier((swap_z(a_blocks), line_z(b_blocks[:, 0])))
    a_held, panels = lax.optimization_barrier((ring_x(a_held), ring_y(b_held)))
    rows_here, slot_all = a_cols.shape
    pattern_slots = c_cols.shape[1]
    block_size = panels.shape[-1]
    slot_of_held = row_slot_of_held(n_row)
    position = jnp.take(lookup(order, a_cols), slot_of_held, axis=1)
    window_col = lookup(b_cols[:, 0], position)
    panel_index = col_held_index(position, per_dev, n_col)
    live_slots = slot_of_held[None, :] < a_lengths[:, None]
    weights = ((window_col[:, :, None] == c_cols[:, None, :]) & live_slots[:, :, None]).astype(
        jnp.float32
    )
    target = jnp.where(jnp.any(weights > 0, axis=-1), jnp.argmax(weights, axis=-1), -1)
    target = target.astype(jnp.int32)
    half = a_held.shape[1]
    mine = row_products(a_held, panels, panel_index[:, :half].reshape(-1),
                        target[:, :half].reshape(-1), pattern_slots)
    return row_products(swap_core(a_held), panels, panel_index[:, half:].reshape(-1),
                        target[:, half:].reshape(-1), pattern_slots, mine)


def split_dot(a, b):
    a_hi = a.astype(jnp.bfloat16)
    a_lo = (a - a_hi.astype(jnp.float32)).astype(jnp.bfloat16)
    b_hi = b.astype(jnp.bfloat16)
    b_lo = (b - b_hi.astype(jnp.float32)).astype(jnp.bfloat16)
    out = jnp.dot(a_hi, b_lo, preferred_element_type=jnp.float32)
    out = out + jnp.dot(a_lo, b_hi, preferred_element_type=jnp.float32)
    return out + jnp.dot(a_hi, b_hi, preferred_element_type=jnp.float32)


def product_kernel(pidx_ref, sidx_ref, a_ref, b_ref, *rest):
    i = pl.program_id(0)
    n_slots = a_ref.shape[1]
    o_ref = rest[-1]
    if len(rest) == 2:
        o_ref[...] = rest[0][...]
    else:
        o_ref[...] = jnp.zeros_like(o_ref)

    def body(j, carry):
        s = sidx_ref[i * n_slots + j]

        @pl.when(s >= 0)
        def _():
            p = pidx_ref[i * n_slots + j]
            prod = split_dot(a_ref[0, j], b_ref[p])
            o_ref[0, s] += prod

        return carry

    lax.fori_loop(0, n_slots, body, 0)


def row_products(whole_slots, panels, panel_index, target, pattern_slots, acc=None, interpret=False):
    rows, slots, bs, _ = whole_slots.shape
    out_spec = pl.BlockSpec((1, pattern_slots, bs, bs), lambda i, pidx, sidx: (i, 0, 0, 0))
    extra = [] if acc is None else [acc]
    grid_spec = pltpu.PrefetchScalarGridSpec(
        num_scalar_prefetch=2,
        grid=(rows,),
        in_specs=[
            pl.BlockSpec((1, slots, bs, bs), lambda i, pidx, sidx: (i, 0, 0, 0)),
            pl.BlockSpec(panels.shape, lambda i, pidx, sidx: (0, 0, 0)),
        ] + [out_spec] * len(extra),
        out_specs=out_spec,
    )
    return pl.pallas_call(
        product_kernel,
        grid_spec=grid_spec,
        out_shape=jax.ShapeDtypeStruct((rows, pattern_slots, bs, bs), jnp.float32),
        input_output_aliases={} if acc is None else {4: 0},
        interpret=interpret,
    )(panel_index, target, whole_slots, panels, *extra)


def solution(mesh):
    sizes = dict(n_row=mesh.shape["row"], n_col=mesh.shape["col"])
    return jax.shard_map(
        functools.partial(local, **sizes),
        mesh=mesh,
        in_specs=(
            P("col", "row", None, None),
            P("col", None),
            P("col"),
            P("col", "row", None, None),
            P(None, "row"),
            P("col", "row"),
            P(),
        ),
        out_specs=P("col", "row", None, None),
        check_vma=False,
    )
```

```python
import functools

import jax
import jax.numpy as jnp
from jax import lax
from jax.experimental import pallas as pl
from jax.experimental.pallas import tpu as pltpu
from jax.sharding import PartitionSpec as P


def lookup(values_table, indices):
    matched = indices[..., None] == jnp.arange(values_table.shape[0], dtype=jnp.int32)
    return jnp.sum(jnp.where(matched, values_table, 0), axis=-1)


def row_stages(n_row):
    n_x = n_row // 4

    def swap_z(chunk):
        pairs = [(r, r ^ 2) for r in range(n_row)]
        return jnp.concatenate([chunk, lax.ppermute(chunk, "row", pairs)], axis=1)

    def ring_x(held):
        parts = [held]
        for k in range(1, n_x):
            shift = [(r, ((r // 4 + k) % n_x) * 4 + r % 4) for r in range(n_row)]
            parts.append(lax.ppermute(held, "row", shift))
        return jnp.concatenate(parts, axis=1)

    def swap_core(held):
        pairs = [(r, r ^ 1) for r in range(n_row)]
        return lax.ppermute(held, "row", pairs)

    return swap_z, ring_x, swap_core


def row_slot_of_held(n_row):
    n_x = n_row // 4
    r = lax.axis_index("row")
    x, zh, core = r // 4, (r // 2) % 2, r % 2
    h = jnp.arange(n_row, dtype=jnp.int32)
    cb, k, zb = h // (2 * n_x), (h // 2) % n_x, h % 2
    return ((x - k) % n_x) * 4 + (zh ^ zb) * 2 + (core ^ cb)


def col_stages(n_col):
    n_y = n_col // 8

    def line_z(chunk):
        c = lax.axis_index("col")
        zl = c % 8
        right = [(c, c + 1) for c in range(n_col) if c % 8 < 7]
        left = [(c, c - 1) for c in range(n_col) if c % 8 > 0]
        from_left, from_right = [chunk], []
        going_right, going_left = chunk, chunk
        for _ in range(7):
            going_right = lax.ppermute(going_right, "col", right)
            going_left = lax.ppermute(going_left, "col", left)
            from_left.append(going_right)
            from_right.append(going_left)
        pieces = jnp.stack(from_left + from_right, axis=0)
        src = jnp.arange(8, dtype=jnp.int32)
        pick = jnp.where(src <= zl, zl - src, 7 + src - zl)
        return jnp.take(pieces, pick, axis=0).reshape((-1,) + chunk.shape[1:])

    def ring_y(held):
        parts = [held]
        for k in range(1, n_y):
            shift = [(c, ((c // 8 + k) % n_y) * 8 + c % 8) for c in range(n_col)]
            parts.append(lax.ppermute(held, "col", shift))
        return jnp.concatenate(parts, axis=0)

    return line_z, ring_y


def col_held_index(grid_pos, per_dev, n_col):
    n_y = n_col // 8
    c = lax.axis_index("col")
    y = c // 8
    src = grid_pos // per_dev
    return ((y - src // 8) % n_y) * (8 * per_dev) + (src % 8) * per_dev + grid_pos % per_dev


def local(a_blocks, a_cols, a_lengths, b_blocks, b_cols, c_cols, order, n_row, n_col):
    per_dev = b_blocks.shape[0]
    swap_z, ring_x, swap_core = row_stages(n_row)
    line_z, ring_y = col_stages(n_col)
    a_held, b_held = lax.optimization_barrier((a_blocks, line_z(b_blocks[:, 0])))
    a_held, b_held = lax.optimization_barrier((swap_z(a_held), b_held))
    a_held, panels = lax.optimization_barrier((ring_x(a_held), ring_y(b_held)))
    rows_here, slot_all = a_cols.shape
    pattern_slots = c_cols.shape[1]
    block_size = panels.shape[-1]
    slot_of_held = row_slot_of_held(n_row)
    position = jnp.take(lookup(order, a_cols), slot_of_held, axis=1)
    window_col = lookup(b_cols[:, 0], position)
    panel_index = col_held_index(position, per_dev, n_col)
    live_slots = slot_of_held[None, :] < a_lengths[:, None]
    weights = ((window_col[:, :, None] == c_cols[:, None, :]) & live_slots[:, :, None]).astype(
        jnp.float32
    )
    target = jnp.where(jnp.any(weights > 0, axis=-1), jnp.argmax(weights, axis=-1), -1)
    target = target.astype(jnp.int32)
    half = a_held.shape[1]
    mine = row_products(a_held, panels, panel_index[:, :half].reshape(-1),
                        target[:, :half].reshape(-1), pattern_slots)
    return row_products(swap_core(a_held), panels, panel_index[:, half:].reshape(-1),
                        target[:, half:].reshape(-1), pattern_slots, mine)


def split_dot(a, b):
    a_hi = a.astype(jnp.bfloat16)
    a_lo = (a - a_hi.astype(jnp.float32)).astype(jnp.bfloat16)
    b_hi = b.astype(jnp.bfloat16)
    b_lo = (b - b_hi.astype(jnp.float32)).astype(jnp.bfloat16)
    out = jnp.dot(a_hi, b_lo, preferred_element_type=jnp.float32)
    out = out + jnp.dot(a_lo, b_hi, preferred_element_type=jnp.float32)
    return out + jnp.dot(a_hi, b_hi, preferred_element_type=jnp.float32)


def product_kernel(pidx_ref, sidx_ref, a_ref, b_ref, *rest):
    i = pl.program_id(0)
    n_slots = a_ref.shape[1]
    o_ref = rest[-1]
    if len(rest) == 2:
        o_ref[...] = rest[0][...]
    else:
        o_ref[...] = jnp.zeros_like(o_ref)

    def body(j, carry):
        s = sidx_ref[i * n_slots + j]

        @pl.when(s >= 0)
        def _():
            p = pidx_ref[i * n_slots + j]
            prod = split_dot(a_ref[0, j], b_ref[p])
            o_ref[0, s] += prod

        return carry

    lax.fori_loop(0, n_slots, body, 0)


def row_products(whole_slots, panels, panel_index, target, pattern_slots, acc=None, interpret=False):
    rows, slots, bs, _ = whole_slots.shape
    out_spec = pl.BlockSpec((1, pattern_slots, bs, bs), lambda i, pidx, sidx: (i, 0, 0, 0))
    extra = [] if acc is None else [acc]
    grid_spec = pltpu.PrefetchScalarGridSpec(
        num_scalar_prefetch=2,
        grid=(rows,),
        in_specs=[
            pl.BlockSpec((1, slots, bs, bs), lambda i, pidx, sidx: (i, 0, 0, 0)),
            pl.BlockSpec(panels.shape, lambda i, pidx, sidx: (0, 0, 0)),
        ] + [out_spec] * len(extra),
        out_specs=out_spec,
    )
    return pl.pallas_call(
        product_kernel,
        grid_spec=grid_spec,
        out_shape=jax.ShapeDtypeStruct((rows, pattern_slots, bs, bs), jnp.float32),
        input_output_aliases={} if acc is None else {4: 0},
        interpret=interpret,
    )(panel_index, target, whole_slots, panels, *extra)


def solution(mesh):
    sizes = dict(n_row=mesh.shape["row"], n_col=mesh.shape["col"])
    return jax.shard_map(
        functools.partial(local, **sizes),
        mesh=mesh,
        in_specs=(
            P("col", "row", None, None),
            P("col", None),
            P("col"),
            P("col", "row", None, None),
            P(None, "row"),
            P("col", "row"),
            P(),
        ),
        out_specs=P("col", "row", None, None),
        check_vma=False,
    )
```

```python
import functools

import jax
import jax.numpy as jnp
from jax import lax
from jax.experimental import pallas as pl
from jax.experimental.pallas import tpu as pltpu
from jax.sharding import PartitionSpec as P


def lookup(values_table, indices):
    matched = indices[..., None] == jnp.arange(values_table.shape[0], dtype=jnp.int32)
    return jnp.sum(jnp.where(matched, values_table, 0), axis=-1)


def row_stages(n_row, n_col):
    n_x = n_row // 4

    def down_z(k):
        r, c = k // n_col, k % n_col
        z = ((r // 2) % 2) * 8 + c % 8 - 4
        z = z % 16
        return ((r // 4) * 4 + (z // 8) * 2 + r % 2) * n_col + (c // 8) * 8 + z % 8

    def swap_z(chunk):
        half = chunk.shape[0] // 2
        pairs = [(r, r ^ 2) for r in range(n_row)]
        direct = lax.ppermute(chunk[:half], "row", pairs)
        legs = [(k, down_z(k)) for k in range(n_row * n_col)]
        around = lax.ppermute(chunk[half:], ("row", "col"), legs)
        around = lax.ppermute(around, ("row", "col"), legs)
        other = jnp.concatenate([direct, around], axis=0)
        return jnp.concatenate([chunk, other], axis=1)

    def ring_x(held):
        parts = [held]
        for k in range(1, n_x):
            shift = [(r, ((r // 4 + k) % n_x) * 4 + r % 4) for r in range(n_row)]
            parts.append(lax.ppermute(held, "row", shift))
        return jnp.concatenate(parts, axis=1)

    def swap_core(held):
        pairs = [(r, r ^ 1) for r in range(n_row)]
        return lax.ppermute(held, "row", pairs)

    return swap_z, ring_x, swap_core


def row_slot_of_held(n_row):
    n_x = n_row // 4
    r = lax.axis_index("row")
    x, zh, core = r // 4, (r // 2) % 2, r % 2
    h = jnp.arange(n_row, dtype=jnp.int32)
    cb, k, zb = h // (2 * n_x), (h // 2) % n_x, h % 2
    return ((x - k) % n_x) * 4 + (zh ^ zb) * 2 + (core ^ cb)


def col_stages(n_col):
    n_y = n_col // 8

    def line_z(chunk):
        c = lax.axis_index("col")
        zl = c % 8
        right = [(c, c + 1) for c in range(n_col) if c % 8 < 7]
        left = [(c, c - 1) for c in range(n_col) if c % 8 > 0]
        from_left, from_right = [chunk], []
        going_right, going_left = chunk, chunk
        for _ in range(7):
            going_right = lax.ppermute(going_right, "col", right)
            going_left = lax.ppermute(going_left, "col", left)
            from_left.append(going_right)
            from_right.append(going_left)
        pieces = jnp.stack(from_left + from_right, axis=0)
        src = jnp.arange(8, dtype=jnp.int32)
        pick = jnp.where(src <= zl, zl - src, 7 + src - zl)
        return jnp.take(pieces, pick, axis=0).reshape((-1,) + chunk.shape[1:])

    def ring_y(held):
        parts = [held]
        for k in range(1, n_y):
            shift = [(c, ((c // 8 + k) % n_y) * 8 + c % 8) for c in range(n_col)]
            parts.append(lax.ppermute(held, "col", shift))
        return jnp.concatenate(parts, axis=0)

    return line_z, ring_y


def col_held_index(grid_pos, per_dev, n_col):
    n_y = n_col // 8
    c = lax.axis_index("col")
    y = c // 8
    src = grid_pos // per_dev
    return ((y - src // 8) % n_y) * (8 * per_dev) + (src % 8) * per_dev + grid_pos % per_dev


def local(a_blocks, a_cols, a_lengths, b_blocks, b_cols, c_cols, order, n_row, n_col):
    per_dev = b_blocks.shape[0]
    swap_z, ring_x, swap_core = row_stages(n_row, n_col)
    line_z, ring_y = col_stages(n_col)
    a_held, b_held = lax.optimization_barrier((a_blocks, line_z(b_blocks[:, 0])))
    a_held, b_held = lax.optimization_barrier((swap_z(a_held), b_held))
    a_held, panels = lax.optimization_barrier((ring_x(a_held), ring_y(b_held)))
    rows_here, slot_all = a_cols.shape
    pattern_slots = c_cols.shape[1]
    block_size = panels.shape[-1]
    slot_of_held = row_slot_of_held(n_row)
    position = jnp.take(lookup(order, a_cols), slot_of_held, axis=1)
    window_col = lookup(b_cols[:, 0], position)
    panel_index = col_held_index(position, per_dev, n_col)
    live_slots = slot_of_held[None, :] < a_lengths[:, None]
    weights = ((window_col[:, :, None] == c_cols[:, None, :]) & live_slots[:, :, None]).astype(
        jnp.float32
    )
    target = jnp.where(jnp.any(weights > 0, axis=-1), jnp.argmax(weights, axis=-1), -1)
    target = target.astype(jnp.int32)
    half = a_held.shape[1]
    mine = row_products(a_held, panels, panel_index[:, :half].reshape(-1),
                        target[:, :half].reshape(-1), pattern_slots)
    return row_products(swap_core(a_held), panels, panel_index[:, half:].reshape(-1),
                        target[:, half:].reshape(-1), pattern_slots, mine)


def split_dot(a, b):
    a_hi = a.astype(jnp.bfloat16)
    a_lo = (a - a_hi.astype(jnp.float32)).astype(jnp.bfloat16)
    b_hi = b.astype(jnp.bfloat16)
    b_lo = (b - b_hi.astype(jnp.float32)).astype(jnp.bfloat16)
    out = jnp.dot(a_hi, b_lo, preferred_element_type=jnp.float32)
    out = out + jnp.dot(a_lo, b_hi, preferred_element_type=jnp.float32)
    return out + jnp.dot(a_hi, b_hi, preferred_element_type=jnp.float32)


def product_kernel(pidx_ref, sidx_ref, a_ref, b_ref, *rest):
    i = pl.program_id(0)
    n_slots = a_ref.shape[1]
    o_ref = rest[-1]
    if len(rest) == 2:
        o_ref[...] = rest[0][...]
    else:
        o_ref[...] = jnp.zeros_like(o_ref)

    def body(j, carry):
        s = sidx_ref[i * n_slots + j]

        @pl.when(s >= 0)
        def _():
            p = pidx_ref[i * n_slots + j]
            prod = split_dot(a_ref[0, j], b_ref[p])
            o_ref[0, s] += prod

        return carry

    lax.fori_loop(0, n_slots, body, 0)


def row_products(whole_slots, panels, panel_index, target, pattern_slots, acc=None, interpret=False):
    rows, slots, bs, _ = whole_slots.shape
    out_spec = pl.BlockSpec((1, pattern_slots, bs, bs), lambda i, pidx, sidx: (i, 0, 0, 0))
    extra = [] if acc is None else [acc]
    grid_spec = pltpu.PrefetchScalarGridSpec(
        num_scalar_prefetch=2,
        grid=(rows,),
        in_specs=[
            pl.BlockSpec((1, slots, bs, bs), lambda i, pidx, sidx: (i, 0, 0, 0)),
            pl.BlockSpec(panels.shape, lambda i, pidx, sidx: (0, 0, 0)),
        ] + [out_spec] * len(extra),
        out_specs=out_spec,
    )
    return pl.pallas_call(
        product_kernel,
        grid_spec=grid_spec,
        out_shape=jax.ShapeDtypeStruct((rows, pattern_slots, bs, bs), jnp.float32),
        input_output_aliases={} if acc is None else {4: 0},
        interpret=interpret,
    )(panel_index, target, whole_slots, panels, *extra)


def solution(mesh):
    sizes = dict(n_row=mesh.shape["row"], n_col=mesh.shape["col"])
    return jax.shard_map(
        functools.partial(local, **sizes),
        mesh=mesh,
        in_specs=(
            P("col", "row", None, None),
            P("col", None),
            P("col"),
            P("col", "row", None, None),
            P(None, "row"),
            P("col", "row"),
            P(),
        ),
        out_specs=P("col", "row", None, None),
        check_vma=False,
    )
```

```python
import functools

import jax
import jax.numpy as jnp
from jax import lax
from jax.experimental import pallas as pl
from jax.experimental.pallas import tpu as pltpu
from jax.sharding import PartitionSpec as P


def lookup(values_table, indices):
    matched = indices[..., None] == jnp.arange(values_table.shape[0], dtype=jnp.int32)
    return jnp.sum(jnp.where(matched, values_table, 0), axis=-1)


def row_stages(n_row):
    n_x = n_row // 4

    def swap_z(chunk):
        pairs = [(r, r ^ 2) for r in range(n_row)]
        return lax.ppermute(chunk, "row", pairs)

    def ring_x(held):
        parts = [held]
        for k in range(1, n_x):
            shift = [(r, ((r // 4 + k) % n_x) * 4 + r % 4) for r in range(n_row)]
            parts.append(lax.ppermute(held, "row", shift))
        return parts

    def swap_core(held):
        pairs = [(r, r ^ 1) for r in range(n_row)]
        return lax.ppermute(held, "row", pairs)

    return swap_z, ring_x, swap_core


def row_slot_of_held(n_row):
    n_x = n_row // 4
    r = lax.axis_index("row")
    x, zh, core = r // 4, (r // 2) % 2, r % 2
    h = jnp.arange(n_row, dtype=jnp.int32)
    cb, k, zb = h // (2 * n_x), (h // 2) % n_x, h % 2
    return ((x - k) % n_x) * 4 + (zh ^ zb) * 2 + (core ^ cb)


def col_stages(n_col):
    n_y = n_col // 8

    def line_z(chunk):
        c = lax.axis_index("col")
        zl = c % 8
        right = [(c, c + 1) for c in range(n_col) if c % 8 < 7]
        left = [(c, c - 1) for c in range(n_col) if c % 8 > 0]
        from_left, from_right = [chunk], []
        going_right, going_left = chunk, chunk
        for _ in range(7):
            going_right = lax.ppermute(going_right, "col", right)
            going_left = lax.ppermute(going_left, "col", left)
            from_left.append(going_right)
            from_right.append(going_left)
        pieces = jnp.stack(from_left + from_right, axis=0)
        src = jnp.arange(8, dtype=jnp.int32)
        pick = jnp.where(src <= zl, zl - src, 7 + src - zl)
        return jnp.take(pieces, pick, axis=0).reshape((-1,) + chunk.shape[1:])

    def ring_y(held):
        parts = [held]
        for k in range(1, n_y):
            shift = [(c, ((c // 8 + k) % n_y) * 8 + c % 8) for c in range(n_col)]
            parts.append(lax.ppermute(held, "col", shift))
        return jnp.concatenate(parts, axis=0)

    return line_z, ring_y


def col_held_index(grid_pos, per_dev, n_col):
    n_y = n_col // 8
    c = lax.axis_index("col")
    y = c // 8
    src = grid_pos // per_dev
    return ((y - src // 8) % n_y) * (8 * per_dev) + (src % 8) * per_dev + grid_pos % per_dev


def local(a_blocks, a_cols, a_lengths, b_blocks, b_cols, c_cols, order, n_row, n_col):
    per_dev = b_blocks.shape[0]
    swap_z, ring_x, swap_core = row_stages(n_row)
    line_z, ring_y = col_stages(n_col)
    a_own, b_held = lax.optimization_barrier((a_blocks, line_z(b_blocks[:, 0])))
    a_other, own_x, panels = lax.optimization_barrier((swap_z(a_own), ring_x(a_own), ring_y(b_held)))
    other_x = ring_x(a_other)
    a_held = jnp.concatenate([p for pair in zip(own_x, other_x) for p in pair], axis=1)
    rows_here, slot_all = a_cols.shape
    pattern_slots = c_cols.shape[1]
    block_size = panels.shape[-1]
    slot_of_held = row_slot_of_held(n_row)
    position = jnp.take(lookup(order, a_cols), slot_of_held, axis=1)
    window_col = lookup(b_cols[:, 0], position)
    panel_index = col_held_index(position, per_dev, n_col)
    live_slots = slot_of_held[None, :] < a_lengths[:, None]
    weights = ((window_col[:, :, None] == c_cols[:, None, :]) & live_slots[:, :, None]).astype(
        jnp.float32
    )
    target = jnp.where(jnp.any(weights > 0, axis=-1), jnp.argmax(weights, axis=-1), -1)
    target = target.astype(jnp.int32)
    half = a_held.shape[1]
    mine = row_products(a_held, panels, panel_index[:, :half].reshape(-1),
                        target[:, :half].reshape(-1), pattern_slots)
    return row_products(swap_core(a_held), panels, panel_index[:, half:].reshape(-1),
                        target[:, half:].reshape(-1), pattern_slots, mine)


def split_dot(a, b):
    a_hi = a.astype(jnp.bfloat16)
    a_lo = (a - a_hi.astype(jnp.float32)).astype(jnp.bfloat16)
    b_hi = b.astype(jnp.bfloat16)
    b_lo = (b - b_hi.astype(jnp.float32)).astype(jnp.bfloat16)
    out = jnp.dot(a_hi, b_lo, preferred_element_type=jnp.float32)
    out = out + jnp.dot(a_lo, b_hi, preferred_element_type=jnp.float32)
    return out + jnp.dot(a_hi, b_hi, preferred_element_type=jnp.float32)


def product_kernel(pidx_ref, sidx_ref, a_ref, b_ref, *rest):
    i = pl.program_id(0)
    n_slots = a_ref.shape[1]
    o_ref = rest[-1]
    if len(rest) == 2:
        o_ref[...] = rest[0][...]
    else:
        o_ref[...] = jnp.zeros_like(o_ref)

    def body(j, carry):
        s = sidx_ref[i * n_slots + j]

        @pl.when(s >= 0)
        def _():
            p = pidx_ref[i * n_slots + j]
            prod = split_dot(a_ref[0, j], b_ref[p])
            o_ref[0, s] += prod

        return carry

    lax.fori_loop(0, n_slots, body, 0)


def row_products(whole_slots, panels, panel_index, target, pattern_slots, acc=None, interpret=False):
    rows, slots, bs, _ = whole_slots.shape
    out_spec = pl.BlockSpec((1, pattern_slots, bs, bs), lambda i, pidx, sidx: (i, 0, 0, 0))
    extra = [] if acc is None else [acc]
    grid_spec = pltpu.PrefetchScalarGridSpec(
        num_scalar_prefetch=2,
        grid=(rows,),
        in_specs=[
            pl.BlockSpec((1, slots, bs, bs), lambda i, pidx, sidx: (i, 0, 0, 0)),
            pl.BlockSpec(panels.shape, lambda i, pidx, sidx: (0, 0, 0)),
        ] + [out_spec] * len(extra),
        out_specs=out_spec,
    )
    return pl.pallas_call(
        product_kernel,
        grid_spec=grid_spec,
        out_shape=jax.ShapeDtypeStruct((rows, pattern_slots, bs, bs), jnp.float32),
        input_output_aliases={} if acc is None else {4: 0},
        interpret=interpret,
    )(panel_index, target, whole_slots, panels, *extra)


def solution(mesh):
    sizes = dict(n_row=mesh.shape["row"], n_col=mesh.shape["col"])
    return jax.shard_map(
        functools.partial(local, **sizes),
        mesh=mesh,
        in_specs=(
            P("col", "row", None, None),
            P("col", None),
            P("col"),
            P("col", "row", None, None),
            P(None, "row"),
            P("col", "row"),
            P(),
        ),
        out_specs=P("col", "row", None, None),
        check_vma=False,
    )
```

```python
import functools

import jax
import jax.numpy as jnp
from jax import lax
from jax.experimental import pallas as pl
from jax.experimental.pallas import tpu as pltpu
from jax.sharding import PartitionSpec as P


def lookup(values_table, indices):
    matched = indices[..., None] == jnp.arange(values_table.shape[0], dtype=jnp.int32)
    return jnp.sum(jnp.where(matched, values_table, 0), axis=-1)


def row_stages(n_row):
    n_x = n_row // 4

    def swap_z(chunk):
        pairs = [(r, r ^ 2) for r in range(n_row)]
        return lax.ppermute(chunk, "row", pairs)

    def ring_x(held):
        parts = [held]
        for k in range(1, n_x):
            shift = [(r, ((r // 4 + k) % n_x) * 4 + r % 4) for r in range(n_row)]
            parts.append(lax.ppermute(held, "row", shift))
        return parts

    def swap_core(held):
        pairs = [(r, r ^ 1) for r in range(n_row)]
        return lax.ppermute(held, "row", pairs)

    return swap_z, ring_x, swap_core


def row_slot_of_held(n_row):
    n_x = n_row // 4
    r = lax.axis_index("row")
    x, zh, core = r // 4, (r // 2) % 2, r % 2
    h = jnp.arange(n_row, dtype=jnp.int32)
    cb, k, zb = h // (2 * n_x), (h // 2) % n_x, h % 2
    return ((x - k) % n_x) * 4 + (zh ^ zb) * 2 + (core ^ cb)


def col_stages(n_col):
    n_y = n_col // 8

    def line_z(chunk):
        c = lax.axis_index("col")
        zl = c % 8
        right = [(c, c + 1) for c in range(n_col) if c % 8 < 7]
        left = [(c, c - 1) for c in range(n_col) if c % 8 > 0]
        from_left, from_right = [chunk], []
        going_right, going_left = chunk, chunk
        for _ in range(7):
            going_right = lax.ppermute(going_right, "col", right)
            going_left = lax.ppermute(going_left, "col", left)
            from_left.append(going_right)
            from_right.append(going_left)
        pieces = jnp.stack(from_left + from_right, axis=0)
        src = jnp.arange(8, dtype=jnp.int32)
        pick = jnp.where(src <= zl, zl - src, 7 + src - zl)
        return jnp.take(pieces, pick, axis=0).reshape((-1,) + chunk.shape[1:])

    def ring_y(held):
        parts = [held]
        for k in range(1, n_y):
            shift = [(c, ((c // 8 + k) % n_y) * 8 + c % 8) for c in range(n_col)]
            parts.append(lax.ppermute(held, "col", shift))
        return jnp.concatenate(parts, axis=0)

    return line_z, ring_y


def col_held_index(grid_pos, per_dev, n_col):
    n_y = n_col // 8
    c = lax.axis_index("col")
    y = c // 8
    src = grid_pos // per_dev
    return ((y - src // 8) % n_y) * (8 * per_dev) + (src % 8) * per_dev + grid_pos % per_dev


def local(a_blocks, a_cols, a_lengths, b_blocks, b_cols, c_cols, order, n_row, n_col):
    per_dev = b_blocks.shape[0]
    swap_z, ring_x, swap_core = row_stages(n_row)
    line_z, ring_y = col_stages(n_col)
    a_own, own_x, b_held = lax.optimization_barrier((a_blocks, ring_x(a_blocks), line_z(b_blocks[:, 0])))
    a_other, panels = lax.optimization_barrier((swap_z(a_own), ring_y(b_held)))
    other_x = ring_x(a_other)
    a_held = jnp.concatenate([p for pair in zip(own_x, other_x) for p in pair], axis=1)
    rows_here, slot_all = a_cols.shape
    pattern_slots = c_cols.shape[1]
    block_size = panels.shape[-1]
    slot_of_held = row_slot_of_held(n_row)
    position = jnp.take(lookup(order, a_cols), slot_of_held, axis=1)
    window_col = lookup(b_cols[:, 0], position)
    panel_index = col_held_index(position, per_dev, n_col)
    live_slots = slot_of_held[None, :] < a_lengths[:, None]
    weights = ((window_col[:, :, None] == c_cols[:, None, :]) & live_slots[:, :, None]).astype(
        jnp.float32
    )
    target = jnp.where(jnp.any(weights > 0, axis=-1), jnp.argmax(weights, axis=-1), -1)
    target = target.astype(jnp.int32)
    half = a_held.shape[1]
    mine = row_products(a_held, panels, panel_index[:, :half].reshape(-1),
                        target[:, :half].reshape(-1), pattern_slots)
    return row_products(swap_core(a_held), panels, panel_index[:, half:].reshape(-1),
                        target[:, half:].reshape(-1), pattern_slots, mine)


def split_dot(a, b):
    a_hi = a.astype(jnp.bfloat16)
    a_lo = (a - a_hi.astype(jnp.float32)).astype(jnp.bfloat16)
    b_hi = b.astype(jnp.bfloat16)
    b_lo = (b - b_hi.astype(jnp.float32)).astype(jnp.bfloat16)
    out = jnp.dot(a_hi, b_lo, preferred_element_type=jnp.float32)
    out = out + jnp.dot(a_lo, b_hi, preferred_element_type=jnp.float32)
    return out + jnp.dot(a_hi, b_hi, preferred_element_type=jnp.float32)


def product_kernel(pidx_ref, sidx_ref, a_ref, b_ref, *rest):
    i = pl.program_id(0)
    n_slots = a_ref.shape[1]
    o_ref = rest[-1]
    if len(rest) == 2:
        o_ref[...] = rest[0][...]
    else:
        o_ref[...] = jnp.zeros_like(o_ref)

    def body(j, carry):
        s = sidx_ref[i * n_slots + j]

        @pl.when(s >= 0)
        def _():
            p = pidx_ref[i * n_slots + j]
            prod = split_dot(a_ref[0, j], b_ref[p])
            o_ref[0, s] += prod

        return carry

    lax.fori_loop(0, n_slots, body, 0)


def row_products(whole_slots, panels, panel_index, target, pattern_slots, acc=None, interpret=False):
    rows, slots, bs, _ = whole_slots.shape
    out_spec = pl.BlockSpec((1, pattern_slots, bs, bs), lambda i, pidx, sidx: (i, 0, 0, 0))
    extra = [] if acc is None else [acc]
    grid_spec = pltpu.PrefetchScalarGridSpec(
        num_scalar_prefetch=2,
        grid=(rows,),
        in_specs=[
            pl.BlockSpec((1, slots, bs, bs), lambda i, pidx, sidx: (i, 0, 0, 0)),
            pl.BlockSpec(panels.shape, lambda i, pidx, sidx: (0, 0, 0)),
        ] + [out_spec] * len(extra),
        out_specs=out_spec,
    )
    return pl.pallas_call(
        product_kernel,
        grid_spec=grid_spec,
        out_shape=jax.ShapeDtypeStruct((rows, pattern_slots, bs, bs), jnp.float32),
        input_output_aliases={} if acc is None else {4: 0},
        interpret=interpret,
    )(panel_index, target, whole_slots, panels, *extra)


def solution(mesh):
    sizes = dict(n_row=mesh.shape["row"], n_col=mesh.shape["col"])
    return jax.shard_map(
        functools.partial(local, **sizes),
        mesh=mesh,
        in_specs=(
            P("col", "row", None, None),
            P("col", None),
            P("col"),
            P("col", "row", None, None),
            P(None, "row"),
            P("col", "row"),
            P(),
        ),
        out_specs=P("col", "row", None, None),
        check_vma=False,
    )
```

```python
import functools

import jax
import jax.numpy as jnp
from jax import lax
from jax.experimental import pallas as pl
from jax.experimental.pallas import tpu as pltpu
from jax.sharding import PartitionSpec as P


def lookup(values_table, indices):
    matched = indices[..., None] == jnp.arange(values_table.shape[0], dtype=jnp.int32)
    return jnp.sum(jnp.where(matched, values_table, 0), axis=-1)


def row_stages(n_row):
    n_x = n_row // 4

    def swap_z(chunk):
        pairs = [(r, r ^ 2) for r in range(n_row)]
        return lax.ppermute(chunk, "row", pairs)

    def ring_x(held):
        parts = [held]
        for k in range(1, n_x):
            shift = [(r, ((r // 4 + k) % n_x) * 4 + r % 4) for r in range(n_row)]
            parts.append(lax.ppermute(held, "row", shift))
        return parts

    def swap_core(held):
        pairs = [(r, r ^ 1) for r in range(n_row)]
        return lax.ppermute(held, "row", pairs)

    return swap_z, ring_x, swap_core


def row_slot_of_held(n_row):
    n_x = n_row // 4
    r = lax.axis_index("row")
    x, zh, core = r // 4, (r // 2) % 2, r % 2
    h = jnp.arange(n_row, dtype=jnp.int32)
    cb, k, zb = h // (2 * n_x), (h // 2) % n_x, h % 2
    return ((x - k) % n_x) * 4 + (zh ^ zb) * 2 + (core ^ cb)


def col_stages(n_col):
    n_y = n_col // 8

    def line_z(chunk):
        c = lax.axis_index("col")
        zl = c % 8
        right = [(c, c + 1) for c in range(n_col) if c % 8 < 7]
        left = [(c, c - 1) for c in range(n_col) if c % 8 > 0]
        from_left, from_right = [chunk], []
        going_right, going_left = chunk, chunk
        for _ in range(7):
            going_right = lax.ppermute(going_right, "col", right)
            going_left = lax.ppermute(going_left, "col", left)
            from_left.append(going_right)
            from_right.append(going_left)
        pieces = jnp.stack(from_left + from_right, axis=0)
        src = jnp.arange(8, dtype=jnp.int32)
        pick = jnp.where(src <= zl, zl - src, 7 + src - zl)
        return jnp.take(pieces, pick, axis=0).reshape((-1,) + chunk.shape[1:])

    def ring_y(held):
        parts = [held]
        for k in range(1, n_y):
            shift = [(c, ((c // 8 + k) % n_y) * 8 + c % 8) for c in range(n_col)]
            parts.append(lax.ppermute(held, "col", shift))
        return jnp.concatenate(parts, axis=0)

    return line_z, ring_y


def col_held_index(grid_pos, per_dev, n_col):
    n_y = n_col // 8
    c = lax.axis_index("col")
    y = c // 8
    src = grid_pos // per_dev
    return ((y - src // 8) % n_y) * (8 * per_dev) + (src % 8) * per_dev + grid_pos % per_dev


def local(a_blocks, a_cols, a_lengths, b_blocks, b_cols, c_cols, order, n_row, n_col):
    per_dev = b_blocks.shape[0]
    swap_z, ring_x, swap_core = row_stages(n_row)
    line_z, ring_y = col_stages(n_col)
    a_own, b_held = lax.optimization_barrier((a_blocks, line_z(b_blocks[:, 0])))
    a_other, own_x, panels = lax.optimization_barrier((swap_z(a_own), ring_x(a_own), ring_y(b_held)))
    other_x = ring_x(a_other)
    a_held = jnp.concatenate([p for pair in zip(own_x, other_x) for p in pair], axis=1)
    rows_here, slot_all = a_cols.shape
    pattern_slots = c_cols.shape[1]
    block_size = panels.shape[-1]
    slot_of_held = row_slot_of_held(n_row)
    position = jnp.take(lookup(order, a_cols), slot_of_held, axis=1)
    window_col = lookup(b_cols[:, 0], position)
    panel_index = col_held_index(position, per_dev, n_col)
    live_slots = slot_of_held[None, :] < a_lengths[:, None]
    weights = ((window_col[:, :, None] == c_cols[:, None, :]) & live_slots[:, :, None]).astype(
        jnp.float32
    )
    target = jnp.where(jnp.any(weights > 0, axis=-1), jnp.argmax(weights, axis=-1), -1)
    target = target.astype(jnp.int32)
    half = a_held.shape[1]

    def products(slots, held_ids, acc=None):
        ids = jnp.array(held_ids, dtype=jnp.int32)
        return row_products(slots, panels, panel_index[:, ids].reshape(-1),
                            target[:, ids].reshape(-1), pattern_slots, acc)

    out = products(jnp.concatenate(own_x, axis=1), list(range(0, half, 2)))
    a_held, out = lax.optimization_barrier((a_held, out))
    out = products(jnp.concatenate(other_x, axis=1), list(range(1, half, 2)), out)
    return products(swap_core(a_held), list(range(half, 2 * half)), out)


def split_dot(a, b):
    a_hi = a.astype(jnp.bfloat16)
    a_lo = (a - a_hi.astype(jnp.float32)).astype(jnp.bfloat16)
    b_hi = b.astype(jnp.bfloat16)
    b_lo = (b - b_hi.astype(jnp.float32)).astype(jnp.bfloat16)
    out = jnp.dot(a_hi, b_lo, preferred_element_type=jnp.float32)
    out = out + jnp.dot(a_lo, b_hi, preferred_element_type=jnp.float32)
    return out + jnp.dot(a_hi, b_hi, preferred_element_type=jnp.float32)


def product_kernel(pidx_ref, sidx_ref, a_ref, b_ref, *rest):
    i = pl.program_id(0)
    n_slots = a_ref.shape[1]
    o_ref = rest[-1]
    if len(rest) == 2:
        o_ref[...] = rest[0][...]
    else:
        o_ref[...] = jnp.zeros_like(o_ref)

    def body(j, carry):
        s = sidx_ref[i * n_slots + j]

        @pl.when(s >= 0)
        def _():
            p = pidx_ref[i * n_slots + j]
            prod = split_dot(a_ref[0, j], b_ref[p])
            o_ref[0, s] += prod

        return carry

    lax.fori_loop(0, n_slots, body, 0)


def row_products(whole_slots, panels, panel_index, target, pattern_slots, acc=None, interpret=False):
    rows, slots, bs, _ = whole_slots.shape
    out_spec = pl.BlockSpec((1, pattern_slots, bs, bs), lambda i, pidx, sidx: (i, 0, 0, 0))
    extra = [] if acc is None else [acc]
    grid_spec = pltpu.PrefetchScalarGridSpec(
        num_scalar_prefetch=2,
        grid=(rows,),
        in_specs=[
            pl.BlockSpec((1, slots, bs, bs), lambda i, pidx, sidx: (i, 0, 0, 0)),
            pl.BlockSpec(panels.shape, lambda i, pidx, sidx: (0, 0, 0)),
        ] + [out_spec] * len(extra),
        out_specs=out_spec,
    )
    return pl.pallas_call(
        product_kernel,
        grid_spec=grid_spec,
        out_shape=jax.ShapeDtypeStruct((rows, pattern_slots, bs, bs), jnp.float32),
        input_output_aliases={} if acc is None else {4: 0},
        interpret=interpret,
    )(panel_index, target, whole_slots, panels, *extra)


def solution(mesh):
    sizes = dict(n_row=mesh.shape["row"], n_col=mesh.shape["col"])
    return jax.shard_map(
        functools.partial(local, **sizes),
        mesh=mesh,
        in_specs=(
            P("col", "row", None, None),
            P("col", None),
            P("col"),
            P("col", "row", None, None),
            P(None, "row"),
            P("col", "row"),
            P(),
        ),
        out_specs=P("col", "row", None, None),
        check_vma=False,
    )
```

```python
import functools

import jax
import jax.numpy as jnp
from jax import lax
from jax.experimental import pallas as pl
from jax.experimental.pallas import tpu as pltpu
from jax.sharding import PartitionSpec as P


def lookup(values_table, indices):
    matched = indices[..., None] == jnp.arange(values_table.shape[0], dtype=jnp.int32)
    return jnp.sum(jnp.where(matched, values_table, 0), axis=-1)


def row_stages(n_row):
    n_x = n_row // 4

    def swap_z(chunk):
        pairs = [(r, r ^ 2) for r in range(n_row)]
        return lax.ppermute(chunk, "row", pairs)

    def ring_x(held):
        parts = [held]
        for k in range(1, n_x):
            shift = [(r, ((r // 4 + k) % n_x) * 4 + r % 4) for r in range(n_row)]
            parts.append(lax.ppermute(held, "row", shift))
        return parts

    def swap_core(held):
        pairs = [(r, r ^ 1) for r in range(n_row)]
        return lax.ppermute(held, "row", pairs)

    return swap_z, ring_x, swap_core


def row_slot_of_held(n_row):
    n_x = n_row // 4
    r = lax.axis_index("row")
    x, zh, core = r // 4, (r // 2) % 2, r % 2
    h = jnp.arange(n_row, dtype=jnp.int32)
    cb, k, zb = h // (2 * n_x), (h // 2) % n_x, h % 2
    return ((x - k) % n_x) * 4 + (zh ^ zb) * 2 + (core ^ cb)


def col_stages(n_col):
    n_y = n_col // 8

    def line_z(chunk):
        c = lax.axis_index("col")
        zl = c % 8
        right = [(c, c + 1) for c in range(n_col) if c % 8 < 7]
        left = [(c, c - 1) for c in range(n_col) if c % 8 > 0]
        from_left, from_right = [chunk], []
        going_right, going_left = chunk, chunk
        for _ in range(7):
            going_right = lax.ppermute(going_right, "col", right)
            going_left = lax.ppermute(going_left, "col", left)
            from_left.append(going_right)
            from_right.append(going_left)
        pieces = jnp.stack(from_left + from_right, axis=0)
        src = jnp.arange(8, dtype=jnp.int32)
        pick = jnp.where(src <= zl, zl - src, 7 + src - zl)
        return jnp.take(pieces, pick, axis=0).reshape((-1,) + chunk.shape[1:])

    def ring_y(held):
        parts = [held]
        for k in range(1, n_y):
            shift = [(c, ((c // 8 + k) % n_y) * 8 + c % 8) for c in range(n_col)]
            parts.append(lax.ppermute(held, "col", shift))
        return jnp.concatenate(parts, axis=0)

    return line_z, ring_y


def col_held_index(grid_pos, per_dev, n_col):
    n_y = n_col // 8
    c = lax.axis_index("col")
    y = c // 8
    src = grid_pos // per_dev
    return ((y - src // 8) % n_y) * (8 * per_dev) + (src % 8) * per_dev + grid_pos % per_dev


def local(a_blocks, a_cols, a_lengths, b_blocks, b_cols, c_cols, order, n_row, n_col):
    per_dev = b_blocks.shape[0]
    swap_z, ring_x, swap_core = row_stages(n_row)
    line_z, ring_y = col_stages(n_col)
    a_own, b_held = lax.optimization_barrier((a_blocks, line_z(b_blocks[:, 0])))
    a_other, own_x, b_held = lax.optimization_barrier((swap_z(a_own), ring_x(a_own), b_held))
    other_x, panels = lax.optimization_barrier((ring_x(a_other), ring_y(b_held)))
    a_held = jnp.concatenate([p for pair in zip(own_x, other_x) for p in pair], axis=1)
    rows_here, slot_all = a_cols.shape
    pattern_slots = c_cols.shape[1]
    block_size = panels.shape[-1]
    slot_of_held = row_slot_of_held(n_row)
    position = jnp.take(lookup(order, a_cols), slot_of_held, axis=1)
    window_col = lookup(b_cols[:, 0], position)
    panel_index = col_held_index(position, per_dev, n_col)
    live_slots = slot_of_held[None, :] < a_lengths[:, None]
    weights = ((window_col[:, :, None] == c_cols[:, None, :]) & live_slots[:, :, None]).astype(
        jnp.float32
    )
    target = jnp.where(jnp.any(weights > 0, axis=-1), jnp.argmax(weights, axis=-1), -1)
    target = target.astype(jnp.int32)
    half = a_held.shape[1]
    mine = row_products(a_held, panels, panel_index[:, :half].reshape(-1),
                        target[:, :half].reshape(-1), pattern_slots)
    return row_products(swap_core(a_held), panels, panel_index[:, half:].reshape(-1),
                        target[:, half:].reshape(-1), pattern_slots, mine)


def split_dot(a, b):
    a_hi = a.astype(jnp.bfloat16)
    a_lo = (a - a_hi.astype(jnp.float32)).astype(jnp.bfloat16)
    b_hi = b.astype(jnp.bfloat16)
    b_lo = (b - b_hi.astype(jnp.float32)).astype(jnp.bfloat16)
    out = jnp.dot(a_hi, b_lo, preferred_element_type=jnp.float32)
    out = out + jnp.dot(a_lo, b_hi, preferred_element_type=jnp.float32)
    return out + jnp.dot(a_hi, b_hi, preferred_element_type=jnp.float32)


def product_kernel(pidx_ref, sidx_ref, a_ref, b_ref, *rest):
    i = pl.program_id(0)
    n_slots = a_ref.shape[1]
    o_ref = rest[-1]
    if len(rest) == 2:
        o_ref[...] = rest[0][...]
    else:
        o_ref[...] = jnp.zeros_like(o_ref)

    def body(j, carry):
        s = sidx_ref[i * n_slots + j]

        @pl.when(s >= 0)
        def _():
            p = pidx_ref[i * n_slots + j]
            prod = split_dot(a_ref[0, j], b_ref[p])
            o_ref[0, s] += prod

        return carry

    lax.fori_loop(0, n_slots, body, 0)


def row_products(whole_slots, panels, panel_index, target, pattern_slots, acc=None, interpret=False):
    rows, slots, bs, _ = whole_slots.shape
    out_spec = pl.BlockSpec((1, pattern_slots, bs, bs), lambda i, pidx, sidx: (i, 0, 0, 0))
    extra = [] if acc is None else [acc]
    grid_spec = pltpu.PrefetchScalarGridSpec(
        num_scalar_prefetch=2,
        grid=(rows,),
        in_specs=[
            pl.BlockSpec((1, slots, bs, bs), lambda i, pidx, sidx: (i, 0, 0, 0)),
            pl.BlockSpec(panels.shape, lambda i, pidx, sidx: (0, 0, 0)),
        ] + [out_spec] * len(extra),
        out_specs=out_spec,
    )
    return pl.pallas_call(
        product_kernel,
        grid_spec=grid_spec,
        out_shape=jax.ShapeDtypeStruct((rows, pattern_slots, bs, bs), jnp.float32),
        input_output_aliases={} if acc is None else {4: 0},
        interpret=interpret,
    )(panel_index, target, whole_slots, panels, *extra)


def solution(mesh):
    sizes = dict(n_row=mesh.shape["row"], n_col=mesh.shape["col"])
    return jax.shard_map(
        functools.partial(local, **sizes),
        mesh=mesh,
        in_specs=(
            P("col", "row", None, None),
            P("col", None),
            P("col"),
            P("col", "row", None, None),
            P(None, "row"),
            P("col", "row"),
            P(),
        ),
        out_specs=P("col", "row", None, None),
        check_vma=False,
    )
```

```python
import functools

import jax
import jax.numpy as jnp
from jax import lax
from jax.experimental import pallas as pl
from jax.experimental.pallas import tpu as pltpu
from jax.sharding import PartitionSpec as P


def lookup(values_table, indices):
    matched = indices[..., None] == jnp.arange(values_table.shape[0], dtype=jnp.int32)
    return jnp.sum(jnp.where(matched, values_table, 0), axis=-1)


def row_stages(n_row):
    n_x = n_row // 4

    def swap_z(chunk):
        pairs = [(r, r ^ 2) for r in range(n_row)]
        return lax.ppermute(chunk, "row", pairs)

    def ring_x(held):
        parts = [held]
        for k in range(1, n_x):
            shift = [(r, ((r // 4 + k) % n_x) * 4 + r % 4) for r in range(n_row)]
            parts.append(lax.ppermute(held, "row", shift))
        return parts

    def swap_core(held):
        pairs = [(r, r ^ 1) for r in range(n_row)]
        return lax.ppermute(held, "row", pairs)

    return swap_z, ring_x, swap_core


def row_slot_of_held(n_row):
    n_x = n_row // 4
    r = lax.axis_index("row")
    x, zh, core = r // 4, (r // 2) % 2, r % 2
    h = jnp.arange(n_row, dtype=jnp.int32)
    cb, k, zb = h // (2 * n_x), (h // 2) % n_x, h % 2
    return ((x - k) % n_x) * 4 + (zh ^ zb) * 2 + (core ^ cb)


def col_stages(n_col):
    n_y = n_col // 8

    def line_z(chunk):
        c = lax.axis_index("col")
        zl = c % 8
        right = [(c, c + 1) for c in range(n_col) if c % 8 < 7]
        left = [(c, c - 1) for c in range(n_col) if c % 8 > 0]
        from_left, from_right = [chunk], []
        going_right, going_left = chunk, chunk
        for _ in range(7):
            going_right = lax.ppermute(going_right, "col", right)
            going_left = lax.ppermute(going_left, "col", left)
            from_left.append(going_right)
            from_right.append(going_left)
        pieces = jnp.stack(from_left + from_right, axis=0)
        src = jnp.arange(8, dtype=jnp.int32)
        pick = jnp.where(src <= zl, zl - src, 7 + src - zl)
        return jnp.take(pieces, pick, axis=0).reshape((-1,) + chunk.shape[1:])

    def ring_y(held):
        parts = [held]
        for k in range(1, n_y):
            shift = [(c, ((c // 8 + k) % n_y) * 8 + c % 8) for c in range(n_col)]
            parts.append(lax.ppermute(held, "col", shift))
        return jnp.concatenate(parts, axis=0)

    return line_z, ring_y


def col_held_index(grid_pos, per_dev, n_col):
    n_y = n_col // 8
    c = lax.axis_index("col")
    y = c // 8
    src = grid_pos // per_dev
    return ((y - src // 8) % n_y) * (8 * per_dev) + (src % 8) * per_dev + grid_pos % per_dev


def local(a_blocks, a_cols, a_lengths, b_blocks, b_cols, c_cols, order, n_row, n_col):
    per_dev = b_blocks.shape[0]
    swap_z, ring_x, swap_core = row_stages(n_row)
    line_z, ring_y = col_stages(n_col)
    a_own, b_held = lax.optimization_barrier((a_blocks, line_z(b_blocks[:, 0])))
    a_other, own_x, panels = lax.optimization_barrier((swap_z(a_own), ring_x(a_own), ring_y(b_held)))
    other_x = ring_x(a_other)
    a_held = jnp.concatenate([p for pair in zip(own_x, other_x) for p in pair], axis=1)
    rows_here, slot_all = a_cols.shape
    pattern_slots = c_cols.shape[1]
    block_size = panels.shape[-1]
    slot_of_held = row_slot_of_held(n_row)
    position = jnp.take(lookup(order, a_cols), slot_of_held, axis=1)
    window_col = lookup(b_cols[:, 0], position)
    panel_index = col_held_index(position, per_dev, n_col)
    live_slots = slot_of_held[None, :] < a_lengths[:, None]
    weights = ((window_col[:, :, None] == c_cols[:, None, :]) & live_slots[:, :, None]).astype(
        jnp.float32
    )
    target = jnp.where(jnp.any(weights > 0, axis=-1), jnp.argmax(weights, axis=-1), -1)
    target = target.astype(jnp.int32)
    half = a_held.shape[1]
    mine = row_products(a_held, panels, panel_index[:, :half].reshape(-1),
                        target[:, :half].reshape(-1), pattern_slots)
    return row_products(swap_core(a_held), panels, panel_index[:, half:].reshape(-1),
                        target[:, half:].reshape(-1), pattern_slots, mine)


def split_dot(a, b):
    a_hi = a.astype(jnp.bfloat16)
    a_lo = (a - a_hi.astype(jnp.float32)).astype(jnp.bfloat16)
    b_hi = b.astype(jnp.bfloat16)
    b_lo = (b - b_hi.astype(jnp.float32)).astype(jnp.bfloat16)
    out = jnp.dot(a_hi, b_lo, preferred_element_type=jnp.float32)
    out = out + jnp.dot(a_lo, b_hi, preferred_element_type=jnp.float32)
    return out + jnp.dot(a_hi, b_hi, preferred_element_type=jnp.float32)


def product_kernel(pidx_ref, sidx_ref, a_ref, b_ref, *rest):
    i = pl.program_id(0)
    n_slots = a_ref.shape[1]
    o_ref = rest[-1]
    if len(rest) == 2:
        o_ref[...] = rest[0][...]
    else:
        o_ref[...] = jnp.zeros_like(o_ref)

    def body(j, carry):
        s = sidx_ref[i * n_slots + j]

        @pl.when(s >= 0)
        def _():
            p = pidx_ref[i * n_slots + j]
            prod = split_dot(a_ref[0, j], b_ref[p])
            o_ref[0, s] += prod

        return carry

    lax.fori_loop(0, n_slots, body, 0, unroll=True)


def row_products(whole_slots, panels, panel_index, target, pattern_slots, acc=None, interpret=False):
    rows, slots, bs, _ = whole_slots.shape
    out_spec = pl.BlockSpec((1, pattern_slots, bs, bs), lambda i, pidx, sidx: (i, 0, 0, 0))
    extra = [] if acc is None else [acc]
    grid_spec = pltpu.PrefetchScalarGridSpec(
        num_scalar_prefetch=2,
        grid=(rows,),
        in_specs=[
            pl.BlockSpec((1, slots, bs, bs), lambda i, pidx, sidx: (i, 0, 0, 0)),
            pl.BlockSpec(panels.shape, lambda i, pidx, sidx: (0, 0, 0)),
        ] + [out_spec] * len(extra),
        out_specs=out_spec,
    )
    return pl.pallas_call(
        product_kernel,
        grid_spec=grid_spec,
        out_shape=jax.ShapeDtypeStruct((rows, pattern_slots, bs, bs), jnp.float32),
        input_output_aliases={} if acc is None else {4: 0},
        interpret=interpret,
    )(panel_index, target, whole_slots, panels, *extra)


def solution(mesh):
    sizes = dict(n_row=mesh.shape["row"], n_col=mesh.shape["col"])
    return jax.shard_map(
        functools.partial(local, **sizes),
        mesh=mesh,
        in_specs=(
            P("col", "row", None, None),
            P("col", None),
            P("col"),
            P("col", "row", None, None),
            P(None, "row"),
            P("col", "row"),
            P(),
        ),
        out_specs=P("col", "row", None, None),
        check_vma=False,
    )
```

```python
import functools

import jax
import jax.numpy as jnp
from jax import lax
from jax.experimental import pallas as pl
from jax.experimental.pallas import tpu as pltpu
from jax.sharding import PartitionSpec as P


def lookup(values_table, indices):
    matched = indices[..., None] == jnp.arange(values_table.shape[0], dtype=jnp.int32)
    return jnp.sum(jnp.where(matched, values_table, 0), axis=-1)


def row_stages(n_row):
    n_x = n_row // 4

    def swap_z(chunk):
        pairs = [(r, r ^ 2) for r in range(n_row)]
        return lax.ppermute(chunk, "row", pairs)

    def ring_x(held):
        parts = [held]
        for k in range(1, n_x):
            shift = [(r, ((r // 4 + k) % n_x) * 4 + r % 4) for r in range(n_row)]
            parts.append(lax.ppermute(held, "row", shift))
        return parts

    def swap_core(held):
        pairs = [(r, r ^ 1) for r in range(n_row)]
        return lax.ppermute(held, "row", pairs)

    return swap_z, ring_x, swap_core


def row_slot_of_held(n_row):
    n_x = n_row // 4
    r = lax.axis_index("row")
    x, zh, core = r // 4, (r // 2) % 2, r % 2
    h = jnp.arange(n_row, dtype=jnp.int32)
    cb, k, zb = h // (2 * n_x), (h // 2) % n_x, h % 2
    return ((x - k) % n_x) * 4 + (zh ^ zb) * 2 + (core ^ cb)


def col_stages(n_col):
    n_y = n_col // 8

    def line_z(chunk):
        c = lax.axis_index("col")
        zl = c % 8
        right = [(c, c + 1) for c in range(n_col) if c % 8 < 7]
        left = [(c, c - 1) for c in range(n_col) if c % 8 > 0]
        from_left, from_right = [chunk], []
        going_right, going_left = chunk, chunk
        for _ in range(7):
            going_right = lax.ppermute(going_right, "col", right)
            going_left = lax.ppermute(going_left, "col", left)
            from_left.append(going_right)
            from_right.append(going_left)
        pieces = jnp.stack(from_left + from_right, axis=0)
        src = jnp.arange(8, dtype=jnp.int32)
        pick = jnp.where(src <= zl, zl - src, 7 + src - zl)
        return jnp.take(pieces, pick, axis=0).reshape((-1,) + chunk.shape[1:])

    def ring_y(held):
        parts = [held]
        for k in range(1, n_y):
            shift = [(c, ((c // 8 + k) % n_y) * 8 + c % 8) for c in range(n_col)]
            parts.append(lax.ppermute(held, "col", shift))
        return jnp.concatenate(parts, axis=0)

    return line_z, ring_y


def col_held_index(grid_pos, per_dev, n_col):
    n_y = n_col // 8
    c = lax.axis_index("col")
    y = c // 8
    src = grid_pos // per_dev
    return ((y - src // 8) % n_y) * (8 * per_dev) + (src % 8) * per_dev + grid_pos % per_dev


def local(a_blocks, a_cols, a_lengths, b_blocks, b_cols, c_cols, order, n_row, n_col):
    per_dev = b_blocks.shape[0]
    swap_z, ring_x, swap_core = row_stages(n_row)
    line_z, ring_y = col_stages(n_col)
    a_own, b_held = lax.optimization_barrier((a_blocks, line_z(b_blocks[:, 0])))
    a_other, own_x, panels = lax.optimization_barrier((swap_z(a_own), ring_x(a_own), ring_y(b_held)))
    own_four = jnp.concatenate(own_x, axis=1)
    other_x, got_own = lax.optimization_barrier((ring_x(a_other), swap_core(own_four)))
    half = 2 * len(own_x)
    rows_here, slot_all = a_cols.shape
    pattern_slots = c_cols.shape[1]
    block_size = panels.shape[-1]
    slot_of_held = row_slot_of_held(n_row)
    position = jnp.take(lookup(order, a_cols), slot_of_held, axis=1)
    window_col = lookup(b_cols[:, 0], position)
    panel_index = col_held_index(position, per_dev, n_col)
    live_slots = slot_of_held[None, :] < a_lengths[:, None]
    weights = ((window_col[:, :, None] == c_cols[:, None, :]) & live_slots[:, :, None]).astype(
        jnp.float32
    )
    target = jnp.where(jnp.any(weights > 0, axis=-1), jnp.argmax(weights, axis=-1), -1)
    target = target.astype(jnp.int32)
    def products(a_list, held_ids, acc=None):
        ids = jnp.array(held_ids, dtype=jnp.int32)
        return row_products(a_list, panels, panel_index[:, ids].reshape(-1),
                            target[:, ids].reshape(-1), pattern_slots, acc)

    order = list(range(0, half, 2)) + list(range(1, half, 2))
    mine = products([own_four] + other_x, order)
    got_other = swap_core(jnp.concatenate(other_x, axis=1))
    return products([got_own, got_other], [half + h for h in order], mine)


def split_dot(a, b):
    a_hi = a.astype(jnp.bfloat16)
    a_lo = (a - a_hi.astype(jnp.float32)).astype(jnp.bfloat16)
    b_hi = b.astype(jnp.bfloat16)
    b_lo = (b - b_hi.astype(jnp.float32)).astype(jnp.bfloat16)
    out = jnp.dot(a_hi, b_lo, preferred_element_type=jnp.float32)
    out = out + jnp.dot(a_lo, b_hi, preferred_element_type=jnp.float32)
    return out + jnp.dot(a_hi, b_hi, preferred_element_type=jnp.float32)


def product_kernel(n_a, pidx_ref, sidx_ref, *refs):
    i = pl.program_id(0)
    a_refs, b_ref, rest = refs[:n_a], refs[n_a], refs[n_a + 1:]
    n_slots = sum(a.shape[1] for a in a_refs)
    o_ref = rest[-1]
    if len(rest) == 2:
        o_ref[...] = rest[0][...]
    else:
        o_ref[...] = jnp.zeros_like(o_ref)
    j = 0
    for a_ref in a_refs:
        for k in range(a_ref.shape[1]):
            s = sidx_ref[i * n_slots + j]

            @pl.when(s >= 0)
            def _():
                p = pidx_ref[i * n_slots + j]
                o_ref[0, s] += split_dot(a_ref[0, k], b_ref[p])

            j += 1


def row_products(a_list, panels, panel_index, target, pattern_slots, acc=None, interpret=False):
    rows, _, bs, _ = a_list[0].shape
    out_spec = pl.BlockSpec((1, pattern_slots, bs, bs), lambda i, pidx, sidx: (i, 0, 0, 0))
    extra = [] if acc is None else [acc]
    a_specs = [pl.BlockSpec((1, a.shape[1], bs, bs), lambda i, pidx, sidx: (i, 0, 0, 0)) for a in a_list]
    grid_spec = pltpu.PrefetchScalarGridSpec(
        num_scalar_prefetch=2,
        grid=(rows,),
        in_specs=a_specs + [
            pl.BlockSpec(panels.shape, lambda i, pidx, sidx: (0, 0, 0)),
        ] + [out_spec] * len(extra),
        out_specs=out_spec,
    )
    return pl.pallas_call(
        functools.partial(product_kernel, len(a_list)),
        grid_spec=grid_spec,
        out_shape=jax.ShapeDtypeStruct((rows, pattern_slots, bs, bs), jnp.float32),
        input_output_aliases={} if acc is None else {3 + len(a_list): 0},
        interpret=interpret,
    )(panel_index, target, *a_list, panels, *extra)


def solution(mesh):
    sizes = dict(n_row=mesh.shape["row"], n_col=mesh.shape["col"])
    return jax.shard_map(
        functools.partial(local, **sizes),
        mesh=mesh,
        in_specs=(
            P("col", "row", None, None),
            P("col", None),
            P("col"),
            P("col", "row", None, None),
            P(None, "row"),
            P("col", "row"),
            P(),
        ),
        out_specs=P("col", "row", None, None),
        check_vma=False,
    )
```

```python
import functools

import jax
import jax.numpy as jnp
from jax import lax
from jax.experimental import pallas as pl
from jax.experimental.pallas import tpu as pltpu
from jax.sharding import PartitionSpec as P


def lookup(values_table, indices):
    matched = indices[..., None] == jnp.arange(values_table.shape[0], dtype=jnp.int32)
    return jnp.sum(jnp.where(matched, values_table, 0), axis=-1)


def row_stages(n_row):
    n_x = n_row // 4

    def swap_z(chunk):
        pairs = [(r, r ^ 2) for r in range(n_row)]
        return lax.ppermute(chunk, "row", pairs)

    def ring_x(held):
        parts = [held]
        for k in range(1, n_x):
            shift = [(r, ((r // 4 + k) % n_x) * 4 + r % 4) for r in range(n_row)]
            parts.append(lax.ppermute(held, "row", shift))
        return parts

    def swap_core(held):
        pairs = [(r, r ^ 1) for r in range(n_row)]
        return lax.ppermute(held, "row", pairs)

    return swap_z, ring_x, swap_core


def row_slot_of_held(n_row):
    n_x = n_row // 4
    r = lax.axis_index("row")
    x, zh, core = r // 4, (r // 2) % 2, r % 2
    h = jnp.arange(n_row, dtype=jnp.int32)
    cb, k, zb = h // (2 * n_x), (h // 2) % n_x, h % 2
    return ((x - k) % n_x) * 4 + (zh ^ zb) * 2 + (core ^ cb)


def col_stages(n_col):
    n_y = n_col // 8

    def line_z(chunk):
        c = lax.axis_index("col")
        zl = c % 8
        right = [(c, c + 1) for c in range(n_col) if c % 8 < 7]
        left = [(c, c - 1) for c in range(n_col) if c % 8 > 0]
        from_left, from_right = [chunk], []
        going_right, going_left = chunk, chunk
        for _ in range(7):
            going_right = lax.ppermute(going_right, "col", right)
            going_left = lax.ppermute(going_left, "col", left)
            from_left.append(going_right)
            from_right.append(going_left)
        pieces = jnp.stack(from_left + from_right, axis=0)
        src = jnp.arange(8, dtype=jnp.int32)
        pick = jnp.where(src <= zl, zl - src, 7 + src - zl)
        return jnp.take(pieces, pick, axis=0).reshape((-1,) + chunk.shape[1:])

    def ring_y(held):
        parts = [held]
        for k in range(1, n_y):
            shift = [(c, ((c // 8 + k) % n_y) * 8 + c % 8) for c in range(n_col)]
            parts.append(lax.ppermute(held, "col", shift))
        return jnp.concatenate(parts, axis=0)

    return line_z, ring_y


def col_held_index(grid_pos, per_dev, n_col):
    n_y = n_col // 8
    c = lax.axis_index("col")
    y = c // 8
    src = grid_pos // per_dev
    return ((y - src // 8) % n_y) * (8 * per_dev) + (src % 8) * per_dev + grid_pos % per_dev


def local(a_blocks, a_cols, a_lengths, b_blocks, b_cols, c_cols, order, n_row, n_col):
    per_dev = b_blocks.shape[0]
    swap_z, ring_x, swap_core = row_stages(n_row)
    line_z, ring_y = col_stages(n_col)
    a_own, b_held = lax.optimization_barrier((a_blocks, line_z(b_blocks[:, 0])))
    a_other, own_x, panels = lax.optimization_barrier((swap_z(a_own), ring_x(a_own), ring_y(b_held)))
    own_four, other_x = lax.optimization_barrier((jnp.concatenate(own_x, axis=1), ring_x(a_other)))
    got_own = swap_core(own_four)
    half = 2 * len(own_x)
    rows_here, slot_all = a_cols.shape
    pattern_slots = c_cols.shape[1]
    block_size = panels.shape[-1]
    slot_of_held = row_slot_of_held(n_row)
    position = jnp.take(lookup(order, a_cols), slot_of_held, axis=1)
    window_col = lookup(b_cols[:, 0], position)
    panel_index = col_held_index(position, per_dev, n_col)
    live_slots = slot_of_held[None, :] < a_lengths[:, None]
    weights = ((window_col[:, :, None] == c_cols[:, None, :]) & live_slots[:, :, None]).astype(
        jnp.float32
    )
    target = jnp.where(jnp.any(weights > 0, axis=-1), jnp.argmax(weights, axis=-1), -1)
    target = target.astype(jnp.int32)
    def products(a_list, held_ids, acc=None):
        ids = jnp.array(held_ids, dtype=jnp.int32)
        return row_products(a_list, panels, panel_index[:, ids].reshape(-1),
                            target[:, ids].reshape(-1), pattern_slots, acc)

    order = list(range(0, half, 2)) + list(range(1, half, 2))
    mine = products([own_four] + other_x, order)
    got_other = swap_core(jnp.concatenate(other_x, axis=1))
    return products([got_own, got_other], [half + h for h in order], mine)


def split_dot(a, b):
    a_hi = a.astype(jnp.bfloat16)
    a_lo = (a - a_hi.astype(jnp.float32)).astype(jnp.bfloat16)
    b_hi = b.astype(jnp.bfloat16)
    b_lo = (b - b_hi.astype(jnp.float32)).astype(jnp.bfloat16)
    out = jnp.dot(a_hi, b_lo, preferred_element_type=jnp.float32)
    out = out + jnp.dot(a_lo, b_hi, preferred_element_type=jnp.float32)
    return out + jnp.dot(a_hi, b_hi, preferred_element_type=jnp.float32)


def product_kernel(n_a, pidx_ref, sidx_ref, *refs):
    i = pl.program_id(0)
    a_refs, b_ref, rest = refs[:n_a], refs[n_a], refs[n_a + 1:]
    n_slots = sum(a.shape[1] for a in a_refs)
    o_ref = rest[-1]
    if len(rest) == 2:
        o_ref[...] = rest[0][...]
    else:
        o_ref[...] = jnp.zeros_like(o_ref)
    j = 0
    for a_ref in a_refs:
        for k in range(a_ref.shape[1]):
            s = sidx_ref[i * n_slots + j]

            @pl.when(s >= 0)
            def _():
                p = pidx_ref[i * n_slots + j]
                o_ref[0, s] += split_dot(a_ref[0, k], b_ref[p])

            j += 1


def row_products(a_list, panels, panel_index, target, pattern_slots, acc=None, interpret=False):
    rows, _, bs, _ = a_list[0].shape
    out_spec = pl.BlockSpec((1, pattern_slots, bs, bs), lambda i, pidx, sidx: (i, 0, 0, 0))
    extra = [] if acc is None else [acc]
    a_specs = [pl.BlockSpec((1, a.shape[1], bs, bs), lambda i, pidx, sidx: (i, 0, 0, 0)) for a in a_list]
    grid_spec = pltpu.PrefetchScalarGridSpec(
        num_scalar_prefetch=2,
        grid=(rows,),
        in_specs=a_specs + [
            pl.BlockSpec(panels.shape, lambda i, pidx, sidx: (0, 0, 0)),
        ] + [out_spec] * len(extra),
        out_specs=out_spec,
    )
    return pl.pallas_call(
        functools.partial(product_kernel, len(a_list)),
        grid_spec=grid_spec,
        out_shape=jax.ShapeDtypeStruct((rows, pattern_slots, bs, bs), jnp.float32),
        input_output_aliases={} if acc is None else {3 + len(a_list): 0},
        interpret=interpret,
    )(panel_index, target, *a_list, panels, *extra)


def solution(mesh):
    sizes = dict(n_row=mesh.shape["row"], n_col=mesh.shape["col"])
    return jax.shard_map(
        functools.partial(local, **sizes),
        mesh=mesh,
        in_specs=(
            P("col", "row", None, None),
            P("col", None),
            P("col"),
            P("col", "row", None, None),
            P(None, "row"),
            P("col", "row"),
            P(),
        ),
        out_specs=P("col", "row", None, None),
        check_vma=False,
    )
```

```python
import functools

import jax
import jax.numpy as jnp
from jax import lax
from jax.experimental import pallas as pl
from jax.experimental.pallas import tpu as pltpu
from jax.sharding import PartitionSpec as P


def lookup(values_table, indices):
    matched = indices[..., None] == jnp.arange(values_table.shape[0], dtype=jnp.int32)
    return jnp.sum(jnp.where(matched, values_table, 0), axis=-1)


def row_stages(n_row):
    n_x = n_row // 4

    def swap_z(chunk):
        pairs = [(r, r ^ 2) for r in range(n_row)]
        return lax.ppermute(chunk, "row", pairs)

    def ring_x(held):
        parts = [held]
        for k in range(1, n_x):
            shift = [(r, ((r // 4 + k) % n_x) * 4 + r % 4) for r in range(n_row)]
            parts.append(lax.ppermute(held, "row", shift))
        return parts

    def swap_core(held):
        pairs = [(r, r ^ 1) for r in range(n_row)]
        return lax.ppermute(held, "row", pairs)

    return swap_z, ring_x, swap_core


def row_slot_of_held(n_row):
    n_x = n_row // 4
    r = lax.axis_index("row")
    x, zh, core = r // 4, (r // 2) % 2, r % 2
    h = jnp.arange(n_row, dtype=jnp.int32)
    cb, k, zb = h // (2 * n_x), (h // 2) % n_x, h % 2
    return ((x - k) % n_x) * 4 + (zh ^ zb) * 2 + (core ^ cb)


def col_stages(n_col):
    n_y = n_col // 8

    def line_z(chunk):
        c = lax.axis_index("col")
        zl = c % 8
        right = [(c, c + 1) for c in range(n_col) if c % 8 < 7]
        left = [(c, c - 1) for c in range(n_col) if c % 8 > 0]
        from_left, from_right = [chunk], []
        going_right, going_left = chunk, chunk
        for _ in range(7):
            going_right = lax.ppermute(going_right, "col", right)
            going_left = lax.ppermute(going_left, "col", left)
            from_left.append(going_right)
            from_right.append(going_left)
        pieces = jnp.stack(from_left + from_right, axis=0)
        src = jnp.arange(8, dtype=jnp.int32)
        pick = jnp.where(src <= zl, zl - src, 7 + src - zl)
        return jnp.take(pieces, pick, axis=0).reshape((-1,) + chunk.shape[1:])

    def ring_y(held):
        parts = [held]
        for k in range(1, n_y):
            shift = [(c, ((c // 8 + k) % n_y) * 8 + c % 8) for c in range(n_col)]
            parts.append(lax.ppermute(held, "col", shift))
        return jnp.concatenate(parts, axis=0)

    return line_z, ring_y


def col_held_index(grid_pos, per_dev, n_col):
    n_y = n_col // 8
    c = lax.axis_index("col")
    y = c // 8
    src = grid_pos // per_dev
    return ((y - src // 8) % n_y) * (8 * per_dev) + (src % 8) * per_dev + grid_pos % per_dev


def local(a_blocks, a_cols, a_lengths, b_blocks, b_cols, c_cols, order, n_row, n_col):
    per_dev = b_blocks.shape[0]
    swap_z, ring_x, swap_core = row_stages(n_row)
    line_z, ring_y = col_stages(n_col)
    a_own, b_held = lax.optimization_barrier((a_blocks, line_z(b_blocks[:, 0])))
    a_other, own_x, panels = lax.optimization_barrier((swap_z(a_own), ring_x(a_own), ring_y(b_held)))
    other_x = ring_x(a_other)
    a_held = jnp.concatenate([p for pair in zip(own_x, other_x) for p in pair], axis=1)
    rows_here, slot_all = a_cols.shape
    pattern_slots = c_cols.shape[1]
    block_size = panels.shape[-1]
    slot_of_held = row_slot_of_held(n_row)
    position = jnp.take(lookup(order, a_cols), slot_of_held, axis=1)
    window_col = lookup(b_cols[:, 0], position)
    panel_index = col_held_index(position, per_dev, n_col)
    live_slots = slot_of_held[None, :] < a_lengths[:, None]
    weights = ((window_col[:, :, None] == c_cols[:, None, :]) & live_slots[:, :, None]).astype(
        jnp.float32
    )
    target = jnp.where(jnp.any(weights > 0, axis=-1), jnp.argmax(weights, axis=-1), -1)
    target = target.astype(jnp.int32)
    half = a_held.shape[1]
    mine = row_products(a_held, panels, panel_index[:, :half].reshape(-1),
                        target[:, :half].reshape(-1), pattern_slots)
    return row_products(swap_core(a_held), panels, panel_index[:, half:].reshape(-1),
                        target[:, half:].reshape(-1), pattern_slots, mine)


def split_dot(a, b):
    a_hi = a.astype(jnp.bfloat16)
    a_lo = (a - a_hi.astype(jnp.float32)).astype(jnp.bfloat16)
    b_hi = b.astype(jnp.bfloat16)
    b_lo = (b - b_hi.astype(jnp.float32)).astype(jnp.bfloat16)
    out = jnp.dot(a_hi, b_lo, preferred_element_type=jnp.float32)
    out = out + jnp.dot(a_lo, b_hi, preferred_element_type=jnp.float32)
    return out + jnp.dot(a_hi, b_hi, preferred_element_type=jnp.float32)


def product_kernel(pidx_ref, sidx_ref, a_ref, b_ref, *rest):
    per_step, n_slots = a_ref.shape[0], a_ref.shape[1]
    o_ref = rest[-1]
    if len(rest) == 2:
        o_ref[...] = rest[0][...]
    else:
        o_ref[...] = jnp.zeros_like(o_ref)

    for r in range(per_step):
        i = pl.program_id(0) * per_step + r

        def body(j, carry):
            s = sidx_ref[i * n_slots + j]

            @pl.when(s >= 0)
            def _():
                p = pidx_ref[i * n_slots + j]
                prod = split_dot(a_ref[r, j], b_ref[p])
                o_ref[r, s] += prod

            return carry

        lax.fori_loop(0, n_slots, body, 0, unroll=True)


def row_products(whole_slots, panels, panel_index, target, pattern_slots, acc=None, interpret=False):
    rows, slots, bs, _ = whole_slots.shape
    per_step = 2 if rows % 2 == 0 else 1
    out_spec = pl.BlockSpec((per_step, pattern_slots, bs, bs), lambda i, pidx, sidx: (i, 0, 0, 0))
    extra = [] if acc is None else [acc]
    grid_spec = pltpu.PrefetchScalarGridSpec(
        num_scalar_prefetch=2,
        grid=(rows // per_step,),
        in_specs=[
            pl.BlockSpec((per_step, slots, bs, bs), lambda i, pidx, sidx: (i, 0, 0, 0)),
            pl.BlockSpec(panels.shape, lambda i, pidx, sidx: (0, 0, 0)),
        ] + [out_spec] * len(extra),
        out_specs=out_spec,
    )
    return pl.pallas_call(
        product_kernel,
        grid_spec=grid_spec,
        out_shape=jax.ShapeDtypeStruct((rows, pattern_slots, bs, bs), jnp.float32),
        input_output_aliases={} if acc is None else {4: 0},
        interpret=interpret,
    )(panel_index, target, whole_slots, panels, *extra)


def solution(mesh):
    sizes = dict(n_row=mesh.shape["row"], n_col=mesh.shape["col"])
    return jax.shard_map(
        functools.partial(local, **sizes),
        mesh=mesh,
        in_specs=(
            P("col", "row", None, None),
            P("col", None),
            P("col"),
            P("col", "row", None, None),
            P(None, "row"),
            P("col", "row"),
            P(),
        ),
        out_specs=P("col", "row", None, None),
        check_vma=False,
    )
```
